32 devices in a mesh: depth: 16 (over z, x, core), gx: 2 (over y).
Axes of the slice: x: 2, y: 2, z: 4, core: 2. Of those that a mesh axis runs over, the one named last changes fastest.
Arguments:
- density: float32 [32, 16, 1024], P('depth', 'gx'), may hold values from 0.25 to 2
- tf_index: int32 [32, 16, 1024], P('depth', 'gx'), may hold values from 0 to 255
- tf_table: float32 [4, 256], replicated, may hold values from 0.3 to 3
Outputs:
- image: float32 [4, 16, 1024], P(None, 'gx', 'depth')
The draws below stay inside these ranges and needn't reach their ends.
All inputs are finite; a program needn't handle non-finite values.
Results may differ from the reference program's by a relative error of at most 0.00011.
Values sent between devices are 32-bit elements; how exact they have to be, the bound alone decides.
No kernel may reach another device: no remote copies, remote signals or barrier semaphores. Data moves between devices by JAX's collectives and lax.ppermute only.
A program may use at most 64 MiB of HBM per device.

```python
import math
import jax
import jax.numpy as jnp
from jax import lax

NY = 1024
K = 256
NZ = 32
NX = 16


def with_ends(array, rng, smallest, largest):
    index_at = [jax.random.randint(jax.random.fold_in(rng, axis), (), 0, length) for axis, length in enumerate(array.shape)]
    main_axis = array.shape.index(max(array.shape))
    neighbour = index_at[:main_axis] + [(index_at[main_axis] + 1) % array.shape[main_axis]] + index_at[main_axis + 1:]
    return array.at[tuple(index_at)].set(smallest).at[tuple(neighbour)].set(largest)


def block_scale(own_key, shape, split, least, largest):
    loudness = 1.0
    for position, parts in split:
        steps = jax.random.uniform(jax.random.fold_in(jax.random.fold_in(own_key, 6), position), (parts,), jnp.float32, least / len(split), largest / len(split))
        loudness = loudness * jnp.repeat(jnp.exp(steps), shape[position] // parts).reshape((-1,) + (1,) * (len(shape) - 1 - position))
    return loudness


def setup_inputs(seed: int = 0) -> dict:
    arg_keys = jax.random.split(jax.random.key(seed), 4)
    density = jnp.clip(jnp.exp(math.log(2.0) - 2.0794415 * jax.random.uniform(arg_keys[0], (NZ, NX, NY), jnp.float32) ** block_scale(arg_keys[0], (NZ, NX, NY), ((0, 16), (1, 2)), -0.2, 0.2)), 0.25, 2.0)
    tf_index = with_ends(jax.random.randint(arg_keys[1], (NZ, NX, NY), 0, K), jax.random.fold_in(arg_keys[1], 1), 0, K - 1).astype(jnp.int32)
    tf_table = jnp.clip(jnp.exp(jax.random.uniform(arg_keys[2], (4, K), jnp.float32, math.log(0.3), math.log(3.0))), 0.3, 3.0)
    return dict(density=density, tf_index=tf_index, tf_table=tf_table)


def smooth(value, axis):
    size = value.shape[axis]
    return lax.slice_in_dim(value, 0, size - 2, axis=axis) + 2.0 * lax.slice_in_dim(value, 1, size - 1, axis=axis) + lax.slice_in_dim(value, 2, size, axis=axis)

def differ(value, axis):
    size = value.shape[axis]
    return lax.slice_in_dim(value, 2, size, axis=axis) - lax.slice_in_dim(value, 0, size - 2, axis=axis)

def shade(grad_z, grad_x, grad_y, dens, entry, step_len):
    inverse = lax.rsqrt(grad_z * grad_z + grad_x * grad_x + grad_y * grad_y + 1.0)
    ndl = (0.48 * grad_z + 0.6 * grad_x + 0.64 * grad_y) * inverse
    ndh = (0.86023 * grad_z + 0.34875 * grad_x + 0.372 * grad_y) * inverse
    shine = jnp.maximum(ndh, 0.0)
    shine = shine * shine
    shine = shine * shine
    shine = shine * shine
    lit = 0.3 + 0.6 * jnp.abs(ndl) + 0.4 * shine
    alpha = 1.0 - jnp.exp(-entry[3] * dens * step_len)
    emit = entry[:3] * (alpha * lit)
    return (emit, 1.0 - alpha)

def reference(density, tf_index, tf_table):
    step_len = 1.0 / NZ
    padded = jnp.pad(density, 1)

    def advance(carry, zpos):
        trans, accum = carry
        slabs = lax.dynamic_slice_in_dim(padded, zpos, 3, 0)
        grad_z = smooth(smooth(differ(slabs, 0), 1), 2)[0] / 2.0
        summed = smooth(slabs, 0)
        grad_x = smooth(differ(summed, 1), 2)[0] / 2.0
        grad_y = differ(smooth(summed, 1), 2)[0] / 2.0
        dens = lax.dynamic_slice_in_dim(density, zpos, 1, 0)[0]
        index = lax.dynamic_slice_in_dim(tf_index, zpos, 1, 0)[0]
        entry = jnp.take(tf_table, index, axis=1)
        emit, transmit = shade(grad_z, grad_x, grad_y, dens, entry, step_len)
        accum = accum + trans[None] * emit
        trans = trans * transmit
        return ((trans, accum), None)
    start = (jnp.ones((NX, NY), jnp.float32), jnp.zeros((3, NX, NY), jnp.float32))
    (trans, accum), _ = lax.scan(advance, start, jnp.arange(NZ, dtype=jnp.int32))
    return jnp.concatenate([accum, (1.0 - trans)[None]], axis=0)
```

```python
import functools

import jax
import jax.numpy as jnp
from jax import lax
from jax.experimental import pallas as pl
from jax.experimental.pallas import tpu as pltpu
from jax.sharding import PartitionSpec as P

LANES = 128
ROWS = 8
BLOCK = 3 * ROWS
WHOLE = pl.BlockSpec(memory_space=pltpu.VMEM)


def pack_kernel(width, dens_ref, index_ref, out_ref):
    length = dens_ref.shape[2]
    lane = lax.broadcasted_iota(jnp.int32, (ROWS, LANES), 1)
    column = lax.broadcasted_iota(jnp.int32, (ROWS, length), 1)
    dens = [dens_ref[0], dens_ref[1]]
    index = [index_ref[0].astype(jnp.float32), index_ref[1].astype(jnp.float32)]
    before = [jnp.where(column == 0, 0.0, pltpu.roll(d, 1, 1)) for d in dens]
    after = [jnp.where(column == length - 1, 0.0, pltpu.roll(d, length - 1, 1)) for d in dens]

    def block(pair, j):
        start = (width * j) // LANES * LANES
        shift = width * j - start
        layers = []
        for layer, value in enumerate(pair):
            amount = (layer * width - shift) % LANES
            window = value[:, start : start + LANES]
            layers.append(pltpu.roll(window, amount, 1) if amount else window)
        return jnp.where(lane < width, layers[0], layers[1])

    for j in range(length // width):
        out_ref[j, 0:ROWS] = block(dens, j)
        out_ref[j, ROWS : 2 * ROWS] = block(index, j)
        out_ref[j, 2 * ROWS : 3 * ROWS] = jnp.where(
            lane % width == 0, block(before, j), block(after, j)
        )


def edge_kernel(got_ref, low_ref, high_ref):
    low_ref[0] = got_ref[:, 0, :]
    low_ref[1] = got_ref[:, 2 * ROWS, :]
    high_ref[0] = got_ref[:, ROWS - 1, :]
    high_ref[1] = got_ref[:, 3 * ROWS - 1, :]


def edge_pick_kernel(got_ref, edge_ref):
    first = lax.axis_index("gx") == 0
    edge_ref[0] = jnp.where(first, got_ref[:, ROWS - 1, :], got_ref[:, 0, :])
    edge_ref[1] = jnp.where(first, got_ref[:, 3 * ROWS - 1, :], got_ref[:, 2 * ROWS, :])


def trade(value, lane, width):
    if 2 * width == LANES:
        return pltpu.roll(value, width, 1)
    return jnp.where(lane < width, pltpu.roll(value, LANES - width, 1), pltpu.roll(value, width, 1))


def render_kernel(width, step_len, paired, got_ref, *refs):
    edge_refs, (table_ref, out_ref) = refs[:-2], refs[-2:]
    bricks = got_ref.shape[0]
    levels = table_ref.shape[1]
    lane = lax.broadcasted_iota(jnp.int32, (ROWS, LANES), 1)
    row = lax.broadcasted_iota(jnp.int32, (ROWS, LANES), 0)
    front_layer = lane < width

    def edge_parts(values):
        brick = lax.broadcasted_iota(jnp.int32, (bricks, LANES), 0)
        edge_lane = lax.broadcasted_iota(jnp.int32, (bricks, LANES), 1)
        other = trade(values, edge_lane, width)
        later = jnp.where(brick == bricks - 1, 0.0, pltpu.roll(other, bricks - 1, 0))
        earlier = jnp.where(brick == 0, 0.0, pltpu.roll(other, 1, 0))
        behind = jnp.where(edge_lane < width, other, later)
        ahead = jnp.where(edge_lane < width, earlier, other)
        return (behind - ahead, ahead + 2.0 * values + behind)

    if paired:
        first = lax.axis_index("gx") == 0
        here = [edge_refs[0][part] for part in range(2)]
        zero = jnp.zeros_like(here[0])
        low = [jnp.where(first, zero, value) for value in here]
        high = [jnp.where(first, value, zero) for value in here]
    else:
        low = [edge_refs[0][part] for part in range(2)]
        high = [edge_refs[1][part] for part in range(2)]
    low = [edge_parts(value) for value in low]
    high = [edge_parts(value) for value in high]

    table = [
        [
            jnp.broadcast_to(table_ref[c : c + 1, start : start + LANES], (ROWS, LANES))
            for start in range(0, levels, LANES)
        ]
        for c in range(4)
    ]

    def lookup(parts, index):
        within = index & (LANES - 1)
        value = jnp.take_along_axis(parts[0], within, axis=1, mode="promise_in_bounds")
        for k in range(1, len(parts)):
            more = jnp.take_along_axis(parts[k], within, axis=1, mode="promise_in_bounds")
            value = jnp.where(index >= k * LANES, more, value)
        return value

    zero = jnp.zeros((ROWS, LANES), jnp.float32)
    dens = [got_ref[k, 0:ROWS] for k in range(bricks)]
    side = [got_ref[k, 2 * ROWS : 3 * ROWS] for k in range(bricks)]
    dens_other = [zero] + [trade(value, lane, width) for value in dens] + [zero]
    side_other = [zero] + [trade(value, lane, width) for value in side] + [zero]

    def depth_parts(value, other, k):
        behind = jnp.where(front_layer, other[k + 1], other[k + 2])
        ahead = jnp.where(front_layer, other[k], other[k + 1])
        return (behind - ahead, ahead + 2.0 * value + behind)

    def across(value, k, part, which):
        below = jnp.where(row == 0, low[part][which][k : k + 1], pltpu.roll(value, 1, 0))
        above = jnp.where(row == ROWS - 1, high[part][which][k : k + 1], pltpu.roll(value, ROWS - 1, 0))
        return below, above

    front = jnp.ones((ROWS, LANES), jnp.float32)
    image = [zero, zero, zero]
    for k in range(bricks):
        planes = []
        for part, (values, other) in enumerate(((dens, dens_other), (side, side_other))):
            delta, total = depth_parts(values[k], other, k)
            below, above = across(delta, k, part, 0)
            for_z = below + 2.0 * delta + above
            below, above = across(total, k, part, 1)
            planes.append((for_z, above - below, below + 2.0 * total + above))

        def beside(which):
            inner, outer = planes[0][which], planes[1][which]
            before = jnp.where(lane % width == 0, outer, pltpu.roll(inner, 1, 1))
            after = jnp.where(lane % width == width - 1, outer, pltpu.roll(inner, LANES - 1, 1))
            return before, inner, after

        before, inner, after = beside(0)
        grad_z = (before + 2.0 * inner + after) * 0.5
        before, inner, after = beside(1)
        grad_x = (before + 2.0 * inner + after) * 0.5
        before, _, after = beside(2)
        grad_y = (after - before) * 0.5

        inverse = lax.rsqrt(grad_z * grad_z + grad_x * grad_x + grad_y * grad_y + 1.0)
        ndl = (0.48 * grad_z + 0.6 * grad_x + 0.64 * grad_y) * inverse
        ndh = (0.86023 * grad_z + 0.34875 * grad_x + 0.372 * grad_y) * inverse
        shine = jnp.maximum(ndh, 0.0)
        shine = shine * shine
        shine = shine * shine
        shine = shine * shine
        lit = 0.3 + 0.6 * jnp.abs(ndl) + 0.4 * shine

        index = got_ref[k, ROWS : 2 * ROWS].astype(jnp.int32)
        alpha = 1.0 - jnp.exp(-lookup(table[3], index) * dens[k] * step_len)
        transmit = 1.0 - alpha
        transmit_other = trade(transmit, lane, width)
        weight = jnp.where(front_layer, front, front * transmit_other) * (alpha * lit)
        image = [image[c] + weight * lookup(table[c], index) for c in range(3)]
        front = front * (transmit * transmit_other)

    for c in range(3):
        out_ref[c] = (image[c] + trade(image[c], lane, width))[:, :width]
    out_ref[3] = (1.0 - front)[:, :width]


def body(density, tf_index, tf_table):
    bricks, ranks = lax.axis_size("depth"), lax.axis_size("gx")
    layers, rows, length = density.shape
    width = length // bricks
    assert layers == 2 and rows == ROWS and 2 * width <= LANES and LANES % width == 0
    step_len = 1.0 / (layers * bricks)
    packed = pl.pallas_call(
        functools.partial(pack_kernel, width),
        out_shape=jax.ShapeDtypeStruct((bricks, BLOCK, LANES), jnp.float32),
        in_specs=[WHOLE] * 2,
        out_specs=WHOLE,
        name="pack",
    )(density, tf_index)
    got = lax.all_to_all(packed, "depth", 0, 0, tiled=True)
    edge = jax.ShapeDtypeStruct((2, bricks, LANES), jnp.float32)
    paired = ranks == 2
    if paired:
        mine = pl.pallas_call(
            edge_pick_kernel, out_shape=edge, in_specs=[WHOLE], out_specs=WHOLE, name="edge"
        )(got)
        edges = [lax.ppermute(mine, "gx", [(0, 1), (1, 0)])]
    else:
        first, last = pl.pallas_call(
            edge_kernel, out_shape=[edge] * 2, in_specs=[WHOLE], out_specs=[WHOLE] * 2, name="edge"
        )(got)
        edges = [
            lax.ppermute(last, "gx", [(i, i + 1) for i in range(ranks - 1)]),
            lax.ppermute(first, "gx", [(i + 1, i) for i in range(ranks - 1)]),
        ]
    return pl.pallas_call(
        functools.partial(render_kernel, width, step_len, paired),
        out_shape=jax.ShapeDtypeStruct((4, rows, width), jnp.float32),
        in_specs=[WHOLE] * (2 + len(edges)),
        out_specs=WHOLE,
        name="render",
    )(got, *edges, tf_table)


def solution(mesh):
    in_specs = (P("depth", "gx", None), P("depth", "gx", None), P())
    out_specs = P(None, "gx", "depth")
    return jax.shard_map(body, mesh=mesh, in_specs=in_specs, out_specs=out_specs, check_vma=False)
```

```python
import functools

import jax
import jax.numpy as jnp
from jax import lax
from jax.experimental import pallas as pl
from jax.experimental.pallas import tpu as pltpu
from jax.sharding import PartitionSpec as P

LANES = 128
ROWS = 8
BLOCK = 3 * ROWS
WHOLE = pl.BlockSpec(memory_space=pltpu.VMEM)
PARAMS = pltpu.CompilerParams(vmem_limit_bytes=4 << 20)


def pack_kernel(width, dens_hbm, index_hbm, out_ref, dens_ref, index_ref, dens_sem, index_sem):
    dens_copy = pltpu.make_async_copy(dens_hbm, dens_ref, dens_sem)
    index_copy = pltpu.make_async_copy(index_hbm, index_ref, index_sem)
    dens_copy.start()
    index_copy.start()
    dens_copy.wait()
    index_copy.wait()
    length = dens_ref.shape[2]
    lane = lax.broadcasted_iota(jnp.int32, (ROWS, LANES), 1)
    column = lax.broadcasted_iota(jnp.int32, (ROWS, length), 1)
    dens = [dens_ref[0], dens_ref[1]]
    index = [index_ref[0].astype(jnp.float32), index_ref[1].astype(jnp.float32)]
    before = [jnp.where(column == 0, 0.0, pltpu.roll(d, 1, 1)) for d in dens]
    after = [jnp.where(column == length - 1, 0.0, pltpu.roll(d, length - 1, 1)) for d in dens]

    def block(pair, j):
        start = (width * j) // LANES * LANES
        shift = width * j - start
        layers = []
        for layer, value in enumerate(pair):
            amount = (layer * width - shift) % LANES
            window = value[:, start : start + LANES]
            layers.append(pltpu.roll(window, amount, 1) if amount else window)
        return jnp.where(lane < width, layers[0], layers[1])

    for j in range(length // width):
        out_ref[j, 0:ROWS] = block(dens, j)
        out_ref[j, ROWS : 2 * ROWS] = block(index, j)
        out_ref[j, 2 * ROWS : 3 * ROWS] = jnp.where(
            lane % width == 0, block(before, j), block(after, j)
        )


def edge_kernel(got_ref, low_ref, high_ref):
    low_ref[0] = got_ref[:, 0, :]
    low_ref[1] = got_ref[:, 2 * ROWS, :]
    high_ref[0] = got_ref[:, ROWS - 1, :]
    high_ref[1] = got_ref[:, 3 * ROWS - 1, :]


def edge_pick_kernel(got_ref, edge_ref):
    first = lax.axis_index("gx") == 0
    edge_ref[0] = jnp.where(first, got_ref[:, ROWS - 1, :], got_ref[:, 0, :])
    edge_ref[1] = jnp.where(first, got_ref[:, 3 * ROWS - 1, :], got_ref[:, 2 * ROWS, :])


def trade(value, lane, width):
    if 2 * width == LANES:
        return pltpu.roll(value, width, 1)
    return jnp.where(lane < width, pltpu.roll(value, LANES - width, 1), pltpu.roll(value, width, 1))


def render_kernel(width, step_len, paired, got_ref, *refs):
    edge_refs, (table_ref, out_ref) = refs[:-2], refs[-2:]
    bricks = got_ref.shape[0]
    levels = table_ref.shape[1]
    lane = lax.broadcasted_iota(jnp.int32, (ROWS, LANES), 1)
    row = lax.broadcasted_iota(jnp.int32, (ROWS, LANES), 0)
    front_layer = lane < width

    def edge_parts(values):
        brick = lax.broadcasted_iota(jnp.int32, (bricks, LANES), 0)
        edge_lane = lax.broadcasted_iota(jnp.int32, (bricks, LANES), 1)
        other = trade(values, edge_lane, width)
        later = jnp.where(brick == bricks - 1, 0.0, pltpu.roll(other, bricks - 1, 0))
        earlier = jnp.where(brick == 0, 0.0, pltpu.roll(other, 1, 0))
        behind = jnp.where(edge_lane < width, other, later)
        ahead = jnp.where(edge_lane < width, earlier, other)
        return (behind - ahead, ahead + 2.0 * values + behind)

    if paired:
        first = lax.axis_index("gx") == 0
        here = [edge_refs[0][part] for part in range(2)]
        zero = jnp.zeros_like(here[0])
        low = [jnp.where(first, zero, value) for value in here]
        high = [jnp.where(first, value, zero) for value in here]
    else:
        low = [edge_refs[0][part] for part in range(2)]
        high = [edge_refs[1][part] for part in range(2)]
    low = [edge_parts(value) for value in low]
    high = [edge_parts(value) for value in high]

    table = [
        [
            jnp.broadcast_to(table_ref[c : c + 1, start : start + LANES], (ROWS, LANES))
            for start in range(0, levels, LANES)
        ]
        for c in range(4)
    ]

    def lookup(parts, index):
        within = index & (LANES - 1)
        value = jnp.take_along_axis(parts[0], within, axis=1, mode="promise_in_bounds")
        for k in range(1, len(parts)):
            more = jnp.take_along_axis(parts[k], within, axis=1, mode="promise_in_bounds")
            value = jnp.where(index >= k * LANES, more, value)
        return value

    zero = jnp.zeros((ROWS, LANES), jnp.float32)
    dens = [got_ref[k, 0:ROWS] for k in range(bricks)]
    side = [got_ref[k, 2 * ROWS : 3 * ROWS] for k in range(bricks)]
    dens_other = [zero] + [trade(value, lane, width) for value in dens] + [zero]
    side_other = [zero] + [trade(value, lane, width) for value in side] + [zero]

    def depth_parts(value, other, k):
        behind = jnp.where(front_layer, other[k + 1], other[k + 2])
        ahead = jnp.where(front_layer, other[k], other[k + 1])
        return (behind - ahead, ahead + 2.0 * value + behind)

    def across(value, k, part, which):
        below = jnp.where(row == 0, low[part][which][k : k + 1], pltpu.roll(value, 1, 0))
        above = jnp.where(row == ROWS - 1, high[part][which][k : k + 1], pltpu.roll(value, ROWS - 1, 0))
        return below, above

    front = jnp.ones((ROWS, LANES), jnp.float32)
    image = [zero, zero, zero]
    for k in range(bricks):
        planes = []
        for part, (values, other) in enumerate(((dens, dens_other), (side, side_other))):
            delta, total = depth_parts(values[k], other, k)
            below, above = across(delta, k, part, 0)
            for_z = below + 2.0 * delta + above
            below, above = across(total, k, part, 1)
            planes.append((for_z, above - below, below + 2.0 * total + above))

        def beside(which):
            inner, outer = planes[0][which], planes[1][which]
            before = jnp.where(lane % width == 0, outer, pltpu.roll(inner, 1, 1))
            after = jnp.where(lane % width == width - 1, outer, pltpu.roll(inner, LANES - 1, 1))
            return before, inner, after

        before, inner, after = beside(0)
        grad_z = (before + 2.0 * inner + after) * 0.5
        before, inner, after = beside(1)
        grad_x = (before + 2.0 * inner + after) * 0.5
        before, _, after = beside(2)
        grad_y = (after - before) * 0.5

        inverse = lax.rsqrt(grad_z * grad_z + grad_x * grad_x + grad_y * grad_y + 1.0)
        ndl = (0.48 * grad_z + 0.6 * grad_x + 0.64 * grad_y) * inverse
        ndh = (0.86023 * grad_z + 0.34875 * grad_x + 0.372 * grad_y) * inverse
        shine = jnp.maximum(ndh, 0.0)
        shine = shine * shine
        shine = shine * shine
        shine = shine * shine
        lit = 0.3 + 0.6 * jnp.abs(ndl) + 0.4 * shine

        index = got_ref[k, ROWS : 2 * ROWS].astype(jnp.int32)
        alpha = 1.0 - jnp.exp(-lookup(table[3], index) * dens[k] * step_len)
        transmit = 1.0 - alpha
        transmit_other = trade(transmit, lane, width)
        weight = jnp.where(front_layer, front, front * transmit_other) * (alpha * lit)
        image = [image[c] + weight * lookup(table[c], index) for c in range(3)]
        front = front * (transmit * transmit_other)

    for c in range(3):
        out_ref[c] = (image[c] + trade(image[c], lane, width))[:, :width]
    out_ref[3] = (1.0 - front)[:, :width]


def body(density, tf_index, tf_table):
    bricks, ranks = lax.axis_size("depth"), lax.axis_size("gx")
    layers, rows, length = density.shape
    width = length // bricks
    assert layers == 2 and rows == ROWS and 2 * width <= LANES and LANES % width == 0
    step_len = 1.0 / (layers * bricks)
    packed = pl.pallas_call(
        functools.partial(pack_kernel, width),
        out_shape=jax.ShapeDtypeStruct((bricks, BLOCK, LANES), jnp.float32),
        in_specs=[pl.BlockSpec(memory_space=pltpu.HBM)] * 2,
        out_specs=WHOLE,
        scratch_shapes=[
            pltpu.VMEM(density.shape, density.dtype),
            pltpu.VMEM(tf_index.shape, tf_index.dtype),
            pltpu.SemaphoreType.DMA,
            pltpu.SemaphoreType.DMA,
        ],
        name="pack", compiler_params=PARAMS,
    )(*(pltpu.with_memory_space_constraint(a, pltpu.HBM) for a in (density, tf_index)))
    got = lax.all_to_all(packed, "depth", 0, 0, tiled=True)
    edge = jax.ShapeDtypeStruct((2, bricks, LANES), jnp.float32)
    paired = ranks == 2
    if paired:
        mine = pl.pallas_call(
            edge_pick_kernel, out_shape=edge, in_specs=[WHOLE], out_specs=WHOLE, name="edge", compiler_params=PARAMS
        )(got)
        edges = [lax.ppermute(mine, "gx", [(0, 1), (1, 0)])]
    else:
        first, last = pl.pallas_call(
            edge_kernel, out_shape=[edge] * 2, in_specs=[WHOLE], out_specs=[WHOLE] * 2, name="edge", compiler_params=PARAMS
        )(got)
        edges = [
            lax.ppermute(last, "gx", [(i, i + 1) for i in range(ranks - 1)]),
            lax.ppermute(first, "gx", [(i + 1, i) for i in range(ranks - 1)]),
        ]
    return pl.pallas_call(
        functools.partial(render_kernel, width, step_len, paired),
        out_shape=jax.ShapeDtypeStruct((4, rows, width), jnp.float32),
        in_specs=[WHOLE] * (2 + len(edges)),
        out_specs=WHOLE,
        name="render", compiler_params=PARAMS,
    )(got, *edges, tf_table)


def solution(mesh):
    in_specs = (P("depth", "gx", None), P("depth", "gx", None), P())
    out_specs = P(None, "gx", "depth")
    return jax.shard_map(body, mesh=mesh, in_specs=in_specs, out_specs=out_specs, check_vma=False)
```

```python
import functools

import jax
import jax.numpy as jnp
from jax import lax
from jax.experimental import pallas as pl
from jax.experimental.pallas import tpu as pltpu
from jax.sharding import PartitionSpec as P

LANES = 128
ROWS = 8
BLOCK = 3 * ROWS
WHOLE = pl.BlockSpec(memory_space=pltpu.VMEM)
PARAMS = pltpu.CompilerParams(vmem_limit_bytes=4 << 20)


def pack_kernel(width, dens_hbm, index_hbm, out_ref, dens_ref, index_ref, dens_sem, index_sem):
    dens_copy = pltpu.make_async_copy(dens_hbm, dens_ref, dens_sem)
    index_copy = pltpu.make_async_copy(index_hbm, index_ref, index_sem)
    dens_copy.start()
    index_copy.start()
    dens_copy.wait()
    index_copy.wait()
    length = dens_ref.shape[2]
    lane = lax.broadcasted_iota(jnp.int32, (ROWS, LANES), 1)
    column = lax.broadcasted_iota(jnp.int32, (ROWS, length), 1)
    dens = [dens_ref[0], dens_ref[1]]
    index = [index_ref[0].astype(jnp.float32), index_ref[1].astype(jnp.float32)]
    before = [jnp.where(column == 0, 0.0, pltpu.roll(d, 1, 1)) for d in dens]
    after = [jnp.where(column == length - 1, 0.0, pltpu.roll(d, length - 1, 1)) for d in dens]

    def block(pair, j):
        start = (width * j) // LANES * LANES
        shift = width * j - start
        layers = []
        for layer, value in enumerate(pair):
            amount = (layer * width - shift) % LANES
            window = value[:, start : start + LANES]
            layers.append(pltpu.roll(window, amount, 1) if amount else window)
        return jnp.where(lane < width, layers[0], layers[1])

    for j in range(length // width):
        out_ref[j, 0:ROWS] = block(dens, j)
        out_ref[j, ROWS : 2 * ROWS] = block(index, j)
        out_ref[j, 2 * ROWS : 3 * ROWS] = jnp.where(
            lane % width == 0, block(before, j), block(after, j)
        )


def edge_kernel(got_ref, low_ref, high_ref):
    low_ref[0] = got_ref[:, 0, :]
    low_ref[1] = got_ref[:, 2 * ROWS, :]
    high_ref[0] = got_ref[:, ROWS - 1, :]
    high_ref[1] = got_ref[:, 3 * ROWS - 1, :]


def edge_pick_kernel(got_ref, edge_ref):
    first = lax.axis_index("gx") == 0
    edge_ref[0] = jnp.where(first, got_ref[:, ROWS - 1, :], got_ref[:, 0, :])
    edge_ref[1] = jnp.where(first, got_ref[:, 3 * ROWS - 1, :], got_ref[:, 2 * ROWS, :])


def trade(value, lane, width):
    if 2 * width == LANES:
        return pltpu.roll(value, width, 1)
    return jnp.where(lane < width, pltpu.roll(value, LANES - width, 1), pltpu.roll(value, width, 1))


def gather_rows(parts, index):
    within = index & (LANES - 1)
    value = jnp.take_along_axis(parts[0], within, axis=1, mode="promise_in_bounds")
    for k in range(1, len(parts)):
        more = jnp.take_along_axis(parts[k], within, axis=1, mode="promise_in_bounds")
        value = jnp.where(index >= k * LANES, more, value)
    return value


def lighting(grad_z, grad_x, grad_y):
    inverse = lax.rsqrt(grad_z * grad_z + grad_x * grad_x + grad_y * grad_y + 1.0)
    ndl = (0.48 * grad_z + 0.6 * grad_x + 0.64 * grad_y) * inverse
    ndh = (0.86023 * grad_z + 0.34875 * grad_x + 0.372 * grad_y) * inverse
    shine = jnp.maximum(ndh, 0.0)
    shine = shine * shine
    shine = shine * shine
    shine = shine * shine
    return 0.3 + 0.6 * jnp.abs(ndl) + 0.4 * shine


def along_y(inner, outer, width):
    lane = lax.broadcasted_iota(jnp.int32, inner.shape, 1)
    before = jnp.where(lane % width == 0, outer, pltpu.roll(inner, 1, 1))
    after = jnp.where(lane % width == width - 1, outer, pltpu.roll(inner, LANES - 1, 1))
    return before, after


def render_kernel(width, step_len, got_ref, table_ref, image_ref, grad_ref, weight_ref):
    bricks = got_ref.shape[0]
    levels = table_ref.shape[1]
    lane = lax.broadcasted_iota(jnp.int32, (ROWS, LANES), 1)
    row = lax.broadcasted_iota(jnp.int32, (ROWS, LANES), 0)
    front_layer = lane < width
    zero = jnp.zeros((ROWS, LANES), jnp.float32)
    table = [
        [
            jnp.broadcast_to(table_ref[c : c + 1, start : start + LANES], (ROWS, LANES))
            for start in range(0, levels, LANES)
        ]
        for c in range(4)
    ]

    def with_ends(values):
        return [zero] + [trade(value, lane, width) for value in values] + [zero]

    dens = [got_ref[k, 0:ROWS] for k in range(bricks)]
    side = [got_ref[k, 2 * ROWS : 3 * ROWS] for k in range(bricks)]
    dens_other, side_other = with_ends(dens), with_ends(side)

    def stencil(value, other, k):
        behind = jnp.where(front_layer, other[k + 1], other[k + 2])
        ahead = jnp.where(front_layer, other[k], other[k + 1])
        planes = (behind - ahead, ahead + 2.0 * value + behind)
        below = [jnp.where(row == 0, 0.0, pltpu.roll(plane, 1, 0)) for plane in planes]
        above = [jnp.where(row == ROWS - 1, 0.0, pltpu.roll(plane, ROWS - 1, 0)) for plane in planes]
        return (
            below[0] + 2.0 * planes[0] + above[0],
            above[1] - below[1],
            below[1] + 2.0 * planes[1] + above[1],
        )

    front = jnp.ones((ROWS, LANES), jnp.float32)
    image = [zero, zero, zero]
    for k in range(bricks):
        inner = stencil(dens[k], dens_other, k)
        outer = stencil(side[k], side_other, k)
        before, after = along_y(inner[0], outer[0], width)
        grad_z = (before + 2.0 * inner[0] + after) * 0.5
        before, after = along_y(inner[1], outer[1], width)
        grad_x = (before + 2.0 * inner[1] + after) * 0.5
        before, after = along_y(inner[2], outer[2], width)
        grad_y = (after - before) * 0.5
        lit = lighting(grad_z, grad_x, grad_y)

        index = got_ref[k, ROWS : 2 * ROWS].astype(jnp.int32)
        alpha = 1.0 - jnp.exp(-gather_rows(table[3], index) * dens[k] * step_len)
        transmit = 1.0 - alpha
        transmit_other = trade(transmit, lane, width)
        seen = jnp.where(front_layer, front, front * transmit_other) * alpha
        front = front * (transmit * transmit_other)
        for part, grad in enumerate((grad_z, grad_x, grad_y)):
            grad_ref[part, k] = grad
        for c in range(3):
            weight = seen * gather_rows(table[c], index)
            weight_ref[c, k] = weight
            image[c] = image[c] + weight * lit

    for c in range(3):
        image_ref[c] = image[c] + trade(image[c], lane, width)
    image_ref[3] = 1.0 - front


def finish_kernel(width, paired, image_ref, grad_ref, weight_ref, *refs):
    edge_refs, out_ref = refs[:-1], refs[-1]
    bricks = grad_ref.shape[1]
    brick = lax.broadcasted_iota(jnp.int32, (bricks, LANES), 0)
    lane = lax.broadcasted_iota(jnp.int32, (bricks, LANES), 1)

    def planes(values):
        other = trade(values, lane, width)
        later = jnp.where(brick == bricks - 1, 0.0, pltpu.roll(other, bricks - 1, 0))
        earlier = jnp.where(brick == 0, 0.0, pltpu.roll(other, 1, 0))
        behind = jnp.where(lane < width, other, later)
        ahead = jnp.where(lane < width, earlier, other)
        return (behind - ahead, ahead + 2.0 * values + behind)

    def outermost(edge_ref, grads, weights, sign):
        delta, total = planes(edge_ref[0])
        delta_side, total_side = planes(edge_ref[1])
        before, after = along_y(delta, delta_side, width)
        grad_z = grads[0] + (before + 2.0 * delta + after) * 0.5
        before, after = along_y(total, total_side, width)
        grad_x = grads[1] + sign * ((before + 2.0 * total + after) * 0.5)
        grad_y = grads[2] + (after - before) * 0.5
        lit = lighting(grad_z, grad_x, grad_y)
        sums = [jnp.sum(weight * lit, axis=0, keepdims=True) for weight in weights]
        return [total + trade(total, lane[:1], width) for total in sums]

    def row_of(ref, row):
        return [ref[part, :, row, :] for part in range(3)]

    row = lax.broadcasted_iota(jnp.int32, (ROWS, width), 0)
    image = [image_ref[c][:, :width] for c in range(3)]
    if paired:
        first = lax.axis_index("gx") == 0
        pick = lambda ref: [
            jnp.where(first, high, low) for high, low in zip(row_of(ref, ROWS - 1), row_of(ref, 0))
        ]
        sign = jnp.where(first, 1.0, -1.0)
        done = outermost(edge_refs[0], pick(grad_ref), pick(weight_ref), sign)
        place = jnp.where(first, ROWS - 1, 0)
        for c in range(3):
            out_ref[c] = jnp.where(row == place, done[c][:, :width], image[c])
    else:
        low = outermost(edge_refs[0], row_of(grad_ref, 0), row_of(weight_ref, 0), -1.0)
        last = ROWS - 1
        high = outermost(edge_refs[1], row_of(grad_ref, last), row_of(weight_ref, last), 1.0)
        for c in range(3):
            value = jnp.where(row == 0, low[c][:, :width], image[c])
            out_ref[c] = jnp.where(row == last, high[c][:, :width], value)
    out_ref[3] = image_ref[3][:, :width]


def body(density, tf_index, tf_table):
    bricks, ranks = lax.axis_size("depth"), lax.axis_size("gx")
    layers, rows, length = density.shape
    width = length // bricks
    assert layers == 2 and rows == ROWS and 2 * width <= LANES and LANES % width == 0
    step_len = 1.0 / (layers * bricks)
    packed = pl.pallas_call(
        functools.partial(pack_kernel, width),
        out_shape=jax.ShapeDtypeStruct((bricks, BLOCK, LANES), jnp.float32),
        in_specs=[pl.BlockSpec(memory_space=pltpu.HBM)] * 2,
        out_specs=WHOLE,
        scratch_shapes=[
            pltpu.VMEM(density.shape, density.dtype),
            pltpu.VMEM(tf_index.shape, tf_index.dtype),
            pltpu.SemaphoreType.DMA,
            pltpu.SemaphoreType.DMA,
        ],
        name="pack", compiler_params=PARAMS,
    )(*(pltpu.with_memory_space_constraint(a, pltpu.HBM) for a in (density, tf_index)))
    got = lax.all_to_all(packed, "depth", 0, 0, tiled=True)
    edge = jax.ShapeDtypeStruct((2, bricks, LANES), jnp.float32)
    paired = ranks == 2
    if paired:
        mine = pl.pallas_call(
            edge_pick_kernel, out_shape=edge, in_specs=[WHOLE], out_specs=WHOLE, name="edge", compiler_params=PARAMS
        )(got)
        edges = [lax.ppermute(mine, "gx", [(0, 1), (1, 0)])]
    else:
        first, last = pl.pallas_call(
            edge_kernel, out_shape=[edge] * 2, in_specs=[WHOLE], out_specs=[WHOLE] * 2, name="edge", compiler_params=PARAMS
        )(got)
        edges = [
            lax.ppermute(last, "gx", [(i, i + 1) for i in range(ranks - 1)]),
            lax.ppermute(first, "gx", [(i + 1, i) for i in range(ranks - 1)]),
        ]
    voxels = jax.ShapeDtypeStruct((3, bricks, ROWS, LANES), jnp.float32)
    parts = pl.pallas_call(
        functools.partial(render_kernel, width, step_len),
        out_shape=[jax.ShapeDtypeStruct((4, ROWS, LANES), jnp.float32), voxels, voxels],
        in_specs=[WHOLE] * 2,
        out_specs=[WHOLE] * 3,
        cost_estimate=pl.CostEstimate(flops=1 << 24, bytes_accessed=1 << 23, transcendentals=0),
        name="render",
        compiler_params=PARAMS,
    )(got, tf_table)
    return pl.pallas_call(
        functools.partial(finish_kernel, width, paired),
        out_shape=jax.ShapeDtypeStruct((4, rows, width), jnp.float32),
        in_specs=[WHOLE] * (3 + len(edges)),
        out_specs=WHOLE,
        name="finish",
        compiler_params=PARAMS,
    )(*parts, *edges)


def solution(mesh):
    in_specs = (P("depth", "gx", None), P("depth", "gx", None), P())
    out_specs = P(None, "gx", "depth")
    return jax.shard_map(body, mesh=mesh, in_specs=in_specs, out_specs=out_specs, check_vma=False)
```

```python
import functools

import jax
import jax.numpy as jnp
from jax import lax
from jax.experimental import pallas as pl
from jax.experimental.pallas import tpu as pltpu
from jax.sharding import PartitionSpec as P

LANES = 128
ROWS = 8
BLOCK = 3 * ROWS
INNER = 4
FAR = (1, 2, 3, 0)
NEAR = (-3, -2, -1, 0)
WHOLE = pl.BlockSpec(memory_space=pltpu.VMEM)
PARAMS = pltpu.CompilerParams(vmem_limit_bytes=4 << 20)


def pack_kernel(width, dens_hbm, index_hbm, out_ref, dens_ref, index_ref, dens_sem, index_sem):
    dens_copy = pltpu.make_async_copy(dens_hbm, dens_ref, dens_sem)
    index_copy = pltpu.make_async_copy(index_hbm, index_ref, index_sem)
    dens_copy.start()
    index_copy.start()
    dens_copy.wait()
    index_copy.wait()
    length = dens_ref.shape[2]
    lane = lax.broadcasted_iota(jnp.int32, (ROWS, LANES), 1)
    column = lax.broadcasted_iota(jnp.int32, (ROWS, length), 1)
    dens = [dens_ref[0], dens_ref[1]]
    index = [index_ref[0].astype(jnp.float32), index_ref[1].astype(jnp.float32)]
    before = [jnp.where(column == 0, 0.0, pltpu.roll(d, 1, 1)) for d in dens]
    after = [jnp.where(column == length - 1, 0.0, pltpu.roll(d, length - 1, 1)) for d in dens]

    def block(pair, j):
        start = (width * j) // LANES * LANES
        shift = width * j - start
        layers = []
        for layer, value in enumerate(pair):
            amount = (layer * width - shift) % LANES
            window = value[:, start : start + LANES]
            layers.append(pltpu.roll(window, amount, 1) if amount else window)
        return jnp.where(lane < width, layers[0], layers[1])

    for j in range(length // width):
        out_ref[j, 0:ROWS] = block(dens, j)
        out_ref[j, ROWS : 2 * ROWS] = block(index, j)
        out_ref[j, 2 * ROWS : 3 * ROWS] = jnp.where(
            lane % width == 0, block(before, j), block(after, j)
        )


def goal(rank, step, count):
    return (rank + step) % count if step >= 0 else rank ^ -step


def origin(rank, step, count):
    return (rank + count - step) % count if step >= 0 else rank ^ -step


def first_kernel(inner, masks, dens_hbm, index_hbm, *refs):
    outs, (dens_ref, index_ref, dens_sem, index_sem) = refs[:-4], refs[-4:]
    groups = len(outs)
    span = dens_ref.shape[2] // groups
    tiles = span // LANES
    dens_copy = pltpu.make_async_copy(dens_hbm, dens_ref, dens_sem)
    index_copy = pltpu.make_async_copy(index_hbm, index_ref, index_sem)
    dens_copy.start()
    index_copy.start()
    mine = lax.axis_index("depth") // inner
    lane = lax.broadcasted_iota(jnp.int32, (ROWS, LANES), 1)
    dens_copy.wait()
    for mask, out_ref in zip(masks, outs):
        group = goal(mine, mask, groups)
        side = jnp.zeros((ROWS, LANES), jnp.float32)
        for layer in range(2):
            for tile in range(tiles):
                start = pl.multiple_of(group * span + tile * LANES, LANES)
                out_ref[layer * tiles + tile] = dens_ref[layer, :, pl.ds(start, LANES)]
            before = pl.multiple_of(jnp.maximum(group * tiles - 1, 0) * LANES, LANES)
            after = pl.multiple_of(jnp.minimum((group + 1) * tiles, groups * tiles - 1) * LANES, LANES)
            left = pltpu.roll(dens_ref[layer, :, pl.ds(before, LANES)], 1 + layer, 1)
            right = pltpu.roll(dens_ref[layer, :, pl.ds(after, LANES)], LANES - 1 - layer, 1)
            side = jnp.where(lane == layer, jnp.where(group == 0, 0.0, left), side)
            side = jnp.where(
                lane == LANES - 1 - layer, jnp.where(group == groups - 1, 0.0, right), side
            )
        out_ref[4 * tiles] = side
    index_copy.wait()
    for mask, out_ref in zip(masks, outs):
        group = goal(mine, mask, groups)
        for layer in range(2):
            for tile in range(tiles):
                start = pl.multiple_of(group * span + tile * LANES, LANES)
                value = index_ref[layer, :, pl.ds(start, LANES)]
                out_ref[(2 + layer) * tiles + tile] = value.astype(jnp.float32)


def second_kernel(width, inner, masks, *refs):
    pieces, outs, scratch = refs[:inner], refs[inner:-1], refs[-1]
    tiles = (pieces[0].shape[0] - 1) // 4
    lane = lax.broadcasted_iota(jnp.int32, (ROWS, LANES), 1)
    side = [jnp.zeros((ROWS, LANES), jnp.float32) for _ in range(inner)]
    for m, piece in enumerate(pieces):
        ends = piece[4 * tiles]
        before, after = [], []
        for layer in range(2):
            value = [piece[layer * tiles + tile] for tile in range(tiles)]
            down = [pltpu.roll(v, 1, 1) for v in value]
            up = [pltpu.roll(v, LANES - 1, 1) for v in value]
            left = pltpu.roll(ends, LANES - layer, 1) if layer else ends
            right = pltpu.roll(ends, layer, 1) if layer else ends
            before.append(
                [jnp.where(lane == 0, d, e) for d, e in zip([left] + down[:-1], down)]
            )
            after.append(
                [jnp.where(lane == LANES - 1, d, e) for d, e in zip(up[1:] + [right], up)]
            )
        dens = [[piece[layer * tiles + tile] for tile in range(tiles)] for layer in range(2)]
        index = [[piece[(2 + layer) * tiles + tile] for tile in range(tiles)] for layer in range(2)]

        def block(pair, t):
            tile, shift = divmod(width * t, LANES)
            layers = []
            for layer, value in enumerate(pair):
                amount = (layer * width - shift) % LANES
                layers.append(pltpu.roll(value[tile], amount, 1) if amount else value[tile])
            return jnp.where(lane < width, layers[0], layers[1])

        for t in range(inner):
            scratch[t, m] = block(dens, t)
            scratch[t, inner + m] = block(index, t)
            first, last = block(before, t), block(after, t)
            first = pltpu.roll(first, m, 1) if m else first
            last = pltpu.roll(last, LANES - m, 1) if m else last
            side[t] = jnp.where(lane % width == m, first, side[t])
            side[t] = jnp.where(lane % width == width - 1 - m, last, side[t])
    for t in range(inner):
        scratch[t, 2 * inner] = side[t]
    mine = lax.axis_index("depth") % inner
    for mask, out_ref in zip(masks, outs):
        out_ref[...] = scratch[goal(mine, mask, inner)]


def arrange_kernel(width, inner, far, near, paired, *refs):
    pieces, (got_ref, edge_refs) = refs[:inner], (refs[inner], refs[inner + 1 :])
    groups = (pieces[0].shape[0] - 1) // 2
    mine = lax.axis_index("depth")
    lane = lax.broadcasted_iota(jnp.int32, (ROWS, LANES), 1)
    for n, piece in zip(near, pieces):
        sides = piece[2 * groups]
        for m in range(groups):
            brick = origin(mine // inner, far[m], groups) * inner + origin(mine % inner, n, inner)
            first = pltpu.roll(sides, LANES - m, 1) if m else sides
            last = pltpu.roll(sides, m, 1) if m else sides
            got_ref[brick, 0:ROWS] = piece[m]
            got_ref[brick, ROWS : 2 * ROWS] = piece[groups + m]
            got_ref[brick, 2 * ROWS : 3 * ROWS] = jnp.where(lane % width == 0, first, last)
    if paired:
        edge_pick_kernel(got_ref, *edge_refs)
    else:
        edge_kernel(got_ref, *edge_refs)


def exchange(values, masks, scale):
    count = lax.axis_size("depth")
    arrived = []
    for value, mask in zip(values, masks):
        rank = lambda i: i // scale % INNER
        pairs = [(i, i + (goal(rank(i), mask, INNER) - rank(i)) * scale) for i in range(count)]
        arrived.append(lax.ppermute(value, "depth", pairs) if mask else value)
    return arrived


def edge_kernel(got_ref, low_ref, high_ref):
    low_ref[0] = got_ref[:, 0, :]
    low_ref[1] = got_ref[:, 2 * ROWS, :]
    high_ref[0] = got_ref[:, ROWS - 1, :]
    high_ref[1] = got_ref[:, 3 * ROWS - 1, :]


def edge_pick_kernel(got_ref, edge_ref):
    first = lax.axis_index("gx") == 0
    edge_ref[0] = jnp.where(first, got_ref[:, ROWS - 1, :], got_ref[:, 0, :])
    edge_ref[1] = jnp.where(first, got_ref[:, 3 * ROWS - 1, :], got_ref[:, 2 * ROWS, :])


def trade(value, lane, width):
    if 2 * width == LANES:
        return pltpu.roll(value, width, 1)
    return jnp.where(lane < width, pltpu.roll(value, LANES - width, 1), pltpu.roll(value, width, 1))


def gather_rows(parts, index):
    within = index & (LANES - 1)
    value = jnp.take_along_axis(parts[0], within, axis=1, mode="promise_in_bounds")
    for k in range(1, len(parts)):
        more = jnp.take_along_axis(parts[k], within, axis=1, mode="promise_in_bounds")
        value = jnp.where(index >= k * LANES, more, value)
    return value


def lighting(grad_z, grad_x, grad_y):
    inverse = lax.rsqrt(grad_z * grad_z + grad_x * grad_x + grad_y * grad_y + 1.0)
    ndl = (0.48 * grad_z + 0.6 * grad_x + 0.64 * grad_y) * inverse
    ndh = (0.86023 * grad_z + 0.34875 * grad_x + 0.372 * grad_y) * inverse
    shine = jnp.maximum(ndh, 0.0)
    shine = shine * shine
    shine = shine * shine
    shine = shine * shine
    return 0.3 + 0.6 * jnp.abs(ndl) + 0.4 * shine


def along_y(inner, outer, width):
    lane = lax.broadcasted_iota(jnp.int32, inner.shape, 1)
    before = jnp.where(lane % width == 0, outer, pltpu.roll(inner, 1, 1))
    after = jnp.where(lane % width == width - 1, outer, pltpu.roll(inner, LANES - 1, 1))
    return before, after


def render_kernel(width, step_len, got_ref, table_ref, image_ref, grad_ref, weight_ref):
    bricks = got_ref.shape[0]
    levels = table_ref.shape[1]
    lane = lax.broadcasted_iota(jnp.int32, (ROWS, LANES), 1)
    row = lax.broadcasted_iota(jnp.int32, (ROWS, LANES), 0)
    front_layer = lane < width
    zero = jnp.zeros((ROWS, LANES), jnp.float32)
    table = [
        [
            jnp.broadcast_to(table_ref[c : c + 1, start : start + LANES], (ROWS, LANES))
            for start in range(0, levels, LANES)
        ]
        for c in range(4)
    ]

    def with_ends(values):
        return [zero] + [trade(value, lane, width) for value in values] + [zero]

    dens = [got_ref[k, 0:ROWS] for k in range(bricks)]
    side = [got_ref[k, 2 * ROWS : 3 * ROWS] for k in range(bricks)]
    dens_other, side_other = with_ends(dens), with_ends(side)

    def stencil(value, other, k):
        behind = jnp.where(front_layer, other[k + 1], other[k + 2])
        ahead = jnp.where(front_layer, other[k], other[k + 1])
        planes = (behind - ahead, ahead + 2.0 * value + behind)
        below = [jnp.where(row == 0, 0.0, pltpu.roll(plane, 1, 0)) for plane in planes]
        above = [jnp.where(row == ROWS - 1, 0.0, pltpu.roll(plane, ROWS - 1, 0)) for plane in planes]
        return (
            below[0] + 2.0 * planes[0] + above[0],
            above[1] - below[1],
            below[1] + 2.0 * planes[1] + above[1],
        )

    front = jnp.ones((ROWS, LANES), jnp.float32)
    image = [zero, zero, zero]
    for k in range(bricks):
        inner = stencil(dens[k], dens_other, k)
        outer = stencil(side[k], side_other, k)
        before, after = along_y(inner[0], outer[0], width)
        grad_z = (before + 2.0 * inner[0] + after) * 0.5
        before, after = along_y(inner[1], outer[1], width)
        grad_x = (before + 2.0 * inner[1] + after) * 0.5
        before, after = along_y(inner[2], outer[2], width)
        grad_y = (after - before) * 0.5
        lit = lighting(grad_z, grad_x, grad_y)

        index = got_ref[k, ROWS : 2 * ROWS].astype(jnp.int32)
        alpha = 1.0 - jnp.exp(-gather_rows(table[3], index) * dens[k] * step_len)
        transmit = 1.0 - alpha
        transmit_other = trade(transmit, lane, width)
        seen = jnp.where(front_layer, front, front * transmit_other) * alpha
        front = front * (transmit * transmit_other)
        for part, grad in enumerate((grad_z, grad_x, grad_y)):
            grad_ref[part, k] = grad
        for c in range(3):
            weight = seen * gather_rows(table[c], index)
            weight_ref[c, k] = weight
            image[c] = image[c] + weight * lit

    for c in range(3):
        image_ref[c] = image[c] + trade(image[c], lane, width)
    image_ref[3] = 1.0 - front


def finish_kernel(width, paired, image_ref, grad_ref, weight_ref, *refs):
    edge_refs, out_ref = refs[:-1], refs[-1]
    bricks = grad_ref.shape[1]
    brick = lax.broadcasted_iota(jnp.int32, (bricks, LANES), 0)
    lane = lax.broadcasted_iota(jnp.int32, (bricks, LANES), 1)

    def planes(values):
        other = trade(values, lane, width)
        later = jnp.where(brick == bricks - 1, 0.0, pltpu.roll(other, bricks - 1, 0))
        earlier = jnp.where(brick == 0, 0.0, pltpu.roll(other, 1, 0))
        behind = jnp.where(lane < width, other, later)
        ahead = jnp.where(lane < width, earlier, other)
        return (behind - ahead, ahead + 2.0 * values + behind)

    def outermost(edge_ref, grads, weights, sign):
        delta, total = planes(edge_ref[0])
        delta_side, total_side = planes(edge_ref[1])
        before, after = along_y(delta, delta_side, width)
        grad_z = grads[0] + (before + 2.0 * delta + after) * 0.5
        before, after = along_y(total, total_side, width)
        grad_x = grads[1] + sign * ((before + 2.0 * total + after) * 0.5)
        grad_y = grads[2] + (after - before) * 0.5
        lit = lighting(grad_z, grad_x, grad_y)
        sums = [jnp.sum(weight * lit, axis=0, keepdims=True) for weight in weights]
        return [total + trade(total, lane[:1], width) for total in sums]

    def row_of(ref, row):
        return [ref[part, :, row, :] for part in range(3)]

    row = lax.broadcasted_iota(jnp.int32, (ROWS, width), 0)
    image = [image_ref[c][:, :width] for c in range(3)]
    if paired:
        first = lax.axis_index("gx") == 0
        pick = lambda ref: [
            jnp.where(first, high, low) for high, low in zip(row_of(ref, ROWS - 1), row_of(ref, 0))
        ]
        sign = jnp.where(first, 1.0, -1.0)
        done = outermost(edge_refs[0], pick(grad_ref), pick(weight_ref), sign)
        place = jnp.where(first, ROWS - 1, 0)
        for c in range(3):
            out_ref[c] = jnp.where(row == place, done[c][:, :width], image[c])
    else:
        low = outermost(edge_refs[0], row_of(grad_ref, 0), row_of(weight_ref, 0), -1.0)
        last = ROWS - 1
        high = outermost(edge_refs[1], row_of(grad_ref, last), row_of(weight_ref, last), 1.0)
        for c in range(3):
            value = jnp.where(row == 0, low[c][:, :width], image[c])
            out_ref[c] = jnp.where(row == last, high[c][:, :width], value)
    out_ref[3] = image_ref[3][:, :width]


def body(density, tf_index, tf_table):
    bricks, ranks = lax.axis_size("depth"), lax.axis_size("gx")
    layers, rows, length = density.shape
    width = length // bricks
    assert layers == 2 and rows == ROWS and 2 * width <= LANES and LANES % width == 0
    step_len = 1.0 / (layers * bricks)
    edge = jax.ShapeDtypeStruct((2, bricks, LANES), jnp.float32)
    paired = ranks == 2
    inputs = [pltpu.with_memory_space_constraint(a, pltpu.HBM) for a in (density, tf_index)]
    landing = [
        pltpu.VMEM(density.shape, density.dtype),
        pltpu.VMEM(tf_index.shape, tf_index.dtype),
        pltpu.SemaphoreType.DMA,
        pltpu.SemaphoreType.DMA,
    ]
    staged = bricks == INNER * INNER and width * INNER % LANES == 0
    if staged:
        tiles = 4 * (width * INNER // LANES) + 1
        sent = pl.pallas_call(
            functools.partial(first_kernel, INNER, FAR),
            out_shape=[jax.ShapeDtypeStruct((tiles, ROWS, LANES), jnp.float32)] * INNER,
            in_specs=[pl.BlockSpec(memory_space=pltpu.HBM)] * 2,
            out_specs=[WHOLE] * INNER,
            scratch_shapes=landing,
            name="first",
            compiler_params=PARAMS,
        )(*inputs)
        pieces = exchange(sent, FAR, INNER)
        tiles = 2 * INNER + 1
        sent = pl.pallas_call(
            functools.partial(second_kernel, width, INNER, NEAR),
            out_shape=[jax.ShapeDtypeStruct((tiles, ROWS, LANES), jnp.float32)] * INNER,
            in_specs=[WHOLE] * INNER,
            out_specs=[WHOLE] * INNER,
            scratch_shapes=[pltpu.VMEM((INNER, tiles, ROWS, LANES), jnp.float32)],
            name="second",
            compiler_params=PARAMS,
        )(*pieces)
        pieces = exchange(sent, NEAR, 1)
        got, *outer = pl.pallas_call(
            functools.partial(arrange_kernel, width, INNER, FAR, NEAR, paired),
            out_shape=[jax.ShapeDtypeStruct((bricks, BLOCK, LANES), jnp.float32)]
            + [edge] * (1 if paired else 2),
            in_specs=[WHOLE] * INNER,
            out_specs=[WHOLE] * (2 if paired else 3),
            name="arrange",
            compiler_params=PARAMS,
        )(*pieces)
    else:
        packed = pl.pallas_call(
            functools.partial(pack_kernel, width),
            out_shape=jax.ShapeDtypeStruct((bricks, BLOCK, LANES), jnp.float32),
            in_specs=[pl.BlockSpec(memory_space=pltpu.HBM)] * 2,
            out_specs=WHOLE,
            scratch_shapes=landing,
            name="pack",
            compiler_params=PARAMS,
        )(*inputs)
        got = lax.all_to_all(packed, "depth", 0, 0, tiled=True)
        outer = pl.pallas_call(
            edge_pick_kernel if paired else edge_kernel,
            out_shape=[edge] * (1 if paired else 2),
            in_specs=[WHOLE],
            out_specs=[WHOLE] * (1 if paired else 2),
            name="edge",
            compiler_params=PARAMS,
        )(got)
    if paired:
        edges = [lax.ppermute(outer[0], "gx", [(0, 1), (1, 0)])]
    else:
        edges = [
            lax.ppermute(outer[1], "gx", [(i, i + 1) for i in range(ranks - 1)]),
            lax.ppermute(outer[0], "gx", [(i + 1, i) for i in range(ranks - 1)]),
        ]
    voxels = jax.ShapeDtypeStruct((3, bricks, ROWS, LANES), jnp.float32)
    parts = pl.pallas_call(
        functools.partial(render_kernel, width, step_len),
        out_shape=[jax.ShapeDtypeStruct((4, ROWS, LANES), jnp.float32), voxels, voxels],
        in_specs=[WHOLE] * 2,
        out_specs=[WHOLE] * 3,
        cost_estimate=pl.CostEstimate(flops=1 << 24, bytes_accessed=1 << 23, transcendentals=0),
        name="render",
        compiler_params=PARAMS,
    )(got, tf_table)
    return pl.pallas_call(
        functools.partial(finish_kernel, width, paired),
        out_shape=jax.ShapeDtypeStruct((4, rows, width), jnp.float32),
        in_specs=[WHOLE] * (3 + len(edges)),
        out_specs=WHOLE,
        name="finish",
        compiler_params=PARAMS,
    )(*parts, *edges)


def solution(mesh):
    in_specs = (P("depth", "gx", None), P("depth", "gx", None), P())
    out_specs = P(None, "gx", "depth")
    return jax.shard_map(body, mesh=mesh, in_specs=in_specs, out_specs=out_specs, check_vma=False)
```

```python
import functools

import jax
import jax.numpy as jnp
from jax import lax
from jax.experimental import pallas as pl
from jax.experimental.pallas import tpu as pltpu
from jax.sharding import PartitionSpec as P

LANES = 128
ROWS = 8
BLOCK = 3 * ROWS
FAR = (1, 2, 3, 0)
WHOLE = pl.BlockSpec(memory_space=pltpu.VMEM)
PARAMS = pltpu.CompilerParams(vmem_limit_bytes=4 << 20)


def pack_kernel(width, dens_hbm, index_hbm, out_ref, dens_ref, index_ref, dens_sem, index_sem):
    dens_copy = pltpu.make_async_copy(dens_hbm, dens_ref, dens_sem)
    index_copy = pltpu.make_async_copy(index_hbm, index_ref, index_sem)
    dens_copy.start()
    index_copy.start()
    dens_copy.wait()
    index_copy.wait()
    length = dens_ref.shape[2]
    lane = lax.broadcasted_iota(jnp.int32, (ROWS, LANES), 1)
    column = lax.broadcasted_iota(jnp.int32, (ROWS, length), 1)
    dens = [dens_ref[0], dens_ref[1]]
    index = [index_ref[0].astype(jnp.float32), index_ref[1].astype(jnp.float32)]
    before = [jnp.where(column == 0, 0.0, pltpu.roll(d, 1, 1)) for d in dens]
    after = [jnp.where(column == length - 1, 0.0, pltpu.roll(d, length - 1, 1)) for d in dens]

    def block(pair, j):
        start = (width * j) // LANES * LANES
        shift = width * j - start
        layers = []
        for layer, value in enumerate(pair):
            amount = (layer * width - shift) % LANES
            window = value[:, start : start + LANES]
            layers.append(pltpu.roll(window, amount, 1) if amount else window)
        return jnp.where(lane < width, layers[0], layers[1])

    for j in range(length // width):
        out_ref[j, 0:ROWS] = block(dens, j)
        out_ref[j, ROWS : 2 * ROWS] = block(index, j)
        out_ref[j, 2 * ROWS : 3 * ROWS] = jnp.where(
            lane % width == 0, block(before, j), block(after, j)
        )


def goal(rank, step, count):
    return (rank + step) % count if step >= 0 else rank ^ -step


def origin(rank, step, count):
    return (rank + count - step) % count if step >= 0 else rank ^ -step


def load_kernel(dens_hbm, index_hbm, dens_ref, index_ref, dens_sem, index_sem):
    dens_copy = pltpu.make_async_copy(dens_hbm, dens_ref, dens_sem)
    index_copy = pltpu.make_async_copy(index_hbm, index_ref, index_sem)
    dens_copy.start()
    index_copy.start()
    dens_copy.wait()
    index_copy.wait()


def first_kernel(*refs):
    own, other, outs, scratch = refs[0:2], refs[2:4], refs[4:-1], refs[-1]
    half = LANES // 2
    mine = lax.axis_index("depth")
    core = mine % 2
    lane = lax.broadcasted_iota(jnp.int32, (ROWS, LANES), 1)
    zero = jnp.zeros((ROWS, LANES), jnp.float32)
    tiles = own[0].shape[2] // LANES
    sides = [zero] * (tiles // 2)

    def tile_of(ref, layer, m):
        return ref[layer, :, m * LANES : (m + 1) * LANES] if 0 <= m < tiles else zero

    def pair(values):
        first = pltpu.roll(values[0], half * core, 1)
        return jnp.where(lane < half, first, pltpu.roll(values[1], half * (1 - core), 1))

    for n, (dens_ref, index_ref) in enumerate((own, other)):
        slot = core ^ n
        for m in range(tiles):
            group, place = divmod(m, 2)
            scratch[group, 4 * place + slot] = pair([tile_of(dens_ref, layer, m) for layer in range(2)])
            scratch[group, 4 * place + 2 + slot] = pair(
                [tile_of(index_ref, layer, m).astype(jnp.float32) for layer in range(2)]
            )
            brick = 2 * place + slot
            for layer in range(2):
                here = tile_of(dens_ref, layer, m)
                before = jnp.where(core == 0, tile_of(dens_ref, layer, m - 1), here)
                after = jnp.where(core == 0, here, tile_of(dens_ref, layer, m + 1))
                at = half * layer + brick
                moved = pltpu.roll(before, (at + 1 + half * core) % LANES, 1)
                sides[group] = jnp.where(lane == at, moved, sides[group])
                at = half * layer + half - 1 - brick
                moved = pltpu.roll(after, (at + half + half * core) % LANES, 1)
                sides[group] = jnp.where(lane == at, moved, sides[group])
    for group, side in enumerate(sides):
        scratch[group, ROWS] = side
    for step, out_ref in zip(FAR, outs):
        out_ref[...] = scratch[goal(mine // 4, step, len(FAR))]


def second_kernel(*refs):
    pieces, (keep_ref, send_ref, near_ref, across_ref, scratch) = refs[: len(FAR)], refs[len(FAR) :]
    half = LANES // 2
    mine = lax.axis_index("depth")
    place = mine // 2 % 2
    lane = lax.broadcasted_iota(jnp.int32, (ROWS, LANES), 1)
    for step, piece in zip(FAR, pieces):
        group = origin(mine // 4, step, len(FAR))
        packed = piece[ROWS]
        for x in range(2):
            for core in range(2):
                brick = 2 * group + core
                p = 2 * x + core
                first = pltpu.roll(packed, LANES - p, 1) if p else packed
                last = pltpu.roll(packed, p, 1) if p else packed
                scratch[x, brick, 0:ROWS] = piece[4 * x + core]
                scratch[x, brick, ROWS : 2 * ROWS] = piece[4 * x + 2 + core]
                scratch[x, brick, 2 * ROWS :] = jnp.where(lane % half == 0, first, last)
    bricks = scratch.shape[1]
    sides = jnp.zeros((ROWS, LANES), jnp.float32)
    for brick in range(bricks):
        keep_ref[brick] = scratch[place, brick]
        send_ref[brick] = scratch[1 - place, brick, 0:ROWS]
        send_ref[bricks + brick] = scratch[1 - place, brick, ROWS : 2 * ROWS]
        side = scratch[1 - place, brick, 2 * ROWS :]
        first = pltpu.roll(side, brick, 1) if brick else side
        last = pltpu.roll(side, LANES - brick, 1) if brick else side
        sides = jnp.where(lane % half == brick, first, sides)
        sides = jnp.where(lane % half == half - 1 - brick, last, sides)
    send_ref[2 * bricks] = sides
    top = lax.axis_index("gx") == 0
    for ref, x in ((near_ref, place), (across_ref, 1 - place)):
        for part in range(2):
            low = 2 * ROWS * part
            ref[part] = jnp.where(top, scratch[x, :, low + ROWS - 1, :], scratch[x, :, low, :])


def staged_render_kernel(width, step_len, keep_ref, came_ref, table_ref, *refs):
    outs, got_ref = refs[:-1], refs[-1]
    half = LANES // 2
    place = lax.axis_index("depth") // 2 % 2
    lane = lax.broadcasted_iota(jnp.int32, (ROWS, LANES), 1)
    bricks = keep_ref.shape[0]
    packed = came_ref[2 * bricks]
    for brick in range(bricks):
        group, core = divmod(brick, 2)
        got_ref[4 * group + 2 * place + core] = keep_ref[brick]
        target = 4 * group + 2 * (1 - place) + core
        first = pltpu.roll(packed, LANES - brick, 1) if brick else packed
        last = pltpu.roll(packed, brick, 1) if brick else packed
        got_ref[target, 0:ROWS] = came_ref[brick]
        got_ref[target, ROWS : 2 * ROWS] = came_ref[bricks + brick]
        got_ref[target, 2 * ROWS :] = jnp.where(lane % half == 0, first, last)
    render_kernel(width, step_len, got_ref, table_ref, *outs)


def staged_finish_kernel(width, image_ref, grad_ref, weight_ref, across_ref, near_ref, out_ref, edge_ref):
    place = lax.axis_index("depth") // 2 % 2
    for part in range(2):
        near, across = near_ref[part], across_ref[part]
        for x, value in enumerate((jnp.where(place == 0, near, across), jnp.where(place == 0, across, near))):
            for group in range(len(FAR)):
                start = 4 * group + 2 * x
                edge_ref[part, start : start + 2] = value[2 * group : 2 * group + 2]
    finish_kernel(width, True, image_ref, grad_ref, weight_ref, edge_ref, out_ref)


def edge_kernel(got_ref, low_ref, high_ref):
    low_ref[0] = got_ref[:, 0, :]
    low_ref[1] = got_ref[:, 2 * ROWS, :]
    high_ref[0] = got_ref[:, ROWS - 1, :]
    high_ref[1] = got_ref[:, 3 * ROWS - 1, :]


def edge_pick_kernel(got_ref, edge_ref):
    first = lax.axis_index("gx") == 0
    edge_ref[0] = jnp.where(first, got_ref[:, ROWS - 1, :], got_ref[:, 0, :])
    edge_ref[1] = jnp.where(first, got_ref[:, 3 * ROWS - 1, :], got_ref[:, 2 * ROWS, :])


def trade(value, lane, width):
    if 2 * width == LANES:
        return pltpu.roll(value, width, 1)
    return jnp.where(lane < width, pltpu.roll(value, LANES - width, 1), pltpu.roll(value, width, 1))


def gather_rows(parts, index):
    within = index & (LANES - 1)
    value = jnp.take_along_axis(parts[0], within, axis=1, mode="promise_in_bounds")
    for k in range(1, len(parts)):
        more = jnp.take_along_axis(parts[k], within, axis=1, mode="promise_in_bounds")
        value = jnp.where(index >= k * LANES, more, value)
    return value


def lighting(grad_z, grad_x, grad_y):
    inverse = lax.rsqrt(grad_z * grad_z + grad_x * grad_x + grad_y * grad_y + 1.0)
    ndl = (0.48 * grad_z + 0.6 * grad_x + 0.64 * grad_y) * inverse
    ndh = (0.86023 * grad_z + 0.34875 * grad_x + 0.372 * grad_y) * inverse
    shine = jnp.maximum(ndh, 0.0)
    shine = shine * shine
    shine = shine * shine
    shine = shine * shine
    return 0.3 + 0.6 * jnp.abs(ndl) + 0.4 * shine


def along_y(inner, outer, width):
    lane = lax.broadcasted_iota(jnp.int32, inner.shape, 1)
    before = jnp.where(lane % width == 0, outer, pltpu.roll(inner, 1, 1))
    after = jnp.where(lane % width == width - 1, outer, pltpu.roll(inner, LANES - 1, 1))
    return before, after


def render_kernel(width, step_len, got_ref, table_ref, image_ref, grad_ref, weight_ref):
    bricks = got_ref.shape[0]
    levels = table_ref.shape[1]
    lane = lax.broadcasted_iota(jnp.int32, (ROWS, LANES), 1)
    row = lax.broadcasted_iota(jnp.int32, (ROWS, LANES), 0)
    front_layer = lane < width
    zero = jnp.zeros((ROWS, LANES), jnp.float32)
    table = [
        [
            jnp.broadcast_to(table_ref[c : c + 1, start : start + LANES], (ROWS, LANES))
            for start in range(0, levels, LANES)
        ]
        for c in range(4)
    ]

    def with_ends(values):
        return [zero] + [trade(value, lane, width) for value in values] + [zero]

    dens = [got_ref[k, 0:ROWS] for k in range(bricks)]
    side = [got_ref[k, 2 * ROWS : 3 * ROWS] for k in range(bricks)]
    dens_other, side_other = with_ends(dens), with_ends(side)

    def stencil(value, other, k):
        behind = jnp.where(front_layer, other[k + 1], other[k + 2])
        ahead = jnp.where(front_layer, other[k], other[k + 1])
        planes = (behind - ahead, ahead + 2.0 * value + behind)
        below = [jnp.where(row == 0, 0.0, pltpu.roll(plane, 1, 0)) for plane in planes]
        above = [jnp.where(row == ROWS - 1, 0.0, pltpu.roll(plane, ROWS - 1, 0)) for plane in planes]
        return (
            below[0] + 2.0 * planes[0] + above[0],
            above[1] - below[1],
            below[1] + 2.0 * planes[1] + above[1],
        )

    front = jnp.ones((ROWS, LANES), jnp.float32)
    image = [zero, zero, zero]
    for k in range(bricks):
        inner = stencil(dens[k], dens_other, k)
        outer = stencil(side[k], side_other, k)
        before, after = along_y(inner[0], outer[0], width)
        grad_z = (before + 2.0 * inner[0] + after) * 0.5
        before, after = along_y(inner[1], outer[1], width)
        grad_x = (before + 2.0 * inner[1] + after) * 0.5
        before, after = along_y(inner[2], outer[2], width)
        grad_y = (after - before) * 0.5
        lit = lighting(grad_z, grad_x, grad_y)

        index = got_ref[k, ROWS : 2 * ROWS].astype(jnp.int32)
        alpha = 1.0 - jnp.exp(-gather_rows(table[3], index) * dens[k] * step_len)
        transmit = 1.0 - alpha
        transmit_other = trade(transmit, lane, width)
        seen = jnp.where(front_layer, front, front * transmit_other) * alpha
        front = front * (transmit * transmit_other)
        for part, grad in enumerate((grad_z, grad_x, grad_y)):
            grad_ref[part, k] = grad
        for c in range(3):
            weight = seen * gather_rows(table[c], index)
            weight_ref[c, k] = weight
            image[c] = image[c] + weight * lit

    for c in range(3):
        image_ref[c] = image[c] + trade(image[c], lane, width)
    image_ref[3] = 1.0 - front


def finish_kernel(width, paired, image_ref, grad_ref, weight_ref, *refs):
    edge_refs, out_ref = refs[:-1], refs[-1]
    bricks = grad_ref.shape[1]
    brick = lax.broadcasted_iota(jnp.int32, (bricks, LANES), 0)
    lane = lax.broadcasted_iota(jnp.int32, (bricks, LANES), 1)

    def planes(values):
        other = trade(values, lane, width)
        later = jnp.where(brick == bricks - 1, 0.0, pltpu.roll(other, bricks - 1, 0))
        earlier = jnp.where(brick == 0, 0.0, pltpu.roll(other, 1, 0))
        behind = jnp.where(lane < width, other, later)
        ahead = jnp.where(lane < width, earlier, other)
        return (behind - ahead, ahead + 2.0 * values + behind)

    def outermost(edge_ref, grads, weights, sign):
        delta, total = planes(edge_ref[0])
        delta_side, total_side = planes(edge_ref[1])
        before, after = along_y(delta, delta_side, width)
        grad_z = grads[0] + (before + 2.0 * delta + after) * 0.5
        before, after = along_y(total, total_side, width)
        grad_x = grads[1] + sign * ((before + 2.0 * total + after) * 0.5)
        grad_y = grads[2] + (after - before) * 0.5
        lit = lighting(grad_z, grad_x, grad_y)
        sums = [jnp.sum(weight * lit, axis=0, keepdims=True) for weight in weights]
        return [total + trade(total, lane[:1], width) for total in sums]

    def row_of(ref, row):
        return [ref[part, :, row, :] for part in range(3)]

    row = lax.broadcasted_iota(jnp.int32, (ROWS, width), 0)
    image = [image_ref[c][:, :width] for c in range(3)]
    if paired:
        first = lax.axis_index("gx") == 0
        pick = lambda ref: [
            jnp.where(first, high, low) for high, low in zip(row_of(ref, ROWS - 1), row_of(ref, 0))
        ]
        sign = jnp.where(first, 1.0, -1.0)
        done = outermost(edge_refs[0], pick(grad_ref), pick(weight_ref), sign)
        place = jnp.where(first, ROWS - 1, 0)
        for c in range(3):
            out_ref[c] = jnp.where(row == place, done[c][:, :width], image[c])
    else:
        low = outermost(edge_refs[0], row_of(grad_ref, 0), row_of(weight_ref, 0), -1.0)
        last = ROWS - 1
        high = outermost(edge_refs[1], row_of(grad_ref, last), row_of(weight_ref, last), 1.0)
        for c in range(3):
            value = jnp.where(row == 0, low[c][:, :width], image[c])
            out_ref[c] = jnp.where(row == last, high[c][:, :width], value)
    out_ref[3] = image_ref[3][:, :width]


def staged_body(density, tf_index, tf_table):
    bricks, groups = lax.axis_size("depth"), len(FAR)
    layers, rows, length = density.shape
    width = length // bricks
    step_len = 1.0 / (layers * bricks)
    half = bricks // 2

    def call(kernel, out_shape, operands, name, scratch=(), cost=None, spec=WHOLE):
        return pl.pallas_call(
            kernel,
            out_shape=out_shape,
            in_specs=[spec] * len(operands),
            out_specs=jax.tree.map(lambda _: WHOLE, out_shape),
            scratch_shapes=scratch,
            cost_estimate=cost,
            name=name,
            compiler_params=PARAMS,
        )(*operands)

    def block(*shape):
        return jax.ShapeDtypeStruct(shape + (ROWS, LANES), jnp.float32)

    def swap(value, mask):
        return lax.ppermute(value, "depth", [(i, i ^ mask) for i in range(bricks)])

    inputs = [pltpu.with_memory_space_constraint(a, pltpu.HBM) for a in (density, tf_index)]
    theirs = [swap(value, 1) for value in (density, tf_index)]
    ours = call(
        load_kernel,
        [jax.ShapeDtypeStruct(a.shape, a.dtype) for a in inputs],
        inputs,
        "load",
        [pltpu.SemaphoreType.DMA] * 2,
        pl.CostEstimate(flops=1 << 20, bytes_accessed=1 << 21, transcendentals=0),
        pl.BlockSpec(memory_space=pltpu.HBM),
    )
    sent = call(
        first_kernel,
        [block(ROWS + 1)] * groups,
        [*ours, *theirs],
        "first",
        [pltpu.VMEM((groups, ROWS + 1, ROWS, LANES), jnp.float32)],
    )
    came = []
    for value, step in zip(sent, FAR):
        pairs = [(i, goal(i // 4, step, groups) * 4 + i % 4) for i in range(bricks)]
        came.append(lax.ppermute(value, "depth", pairs) if step else value)
    edge = jax.ShapeDtypeStruct((2, half, LANES), jnp.float32)
    keep, send, near, across = call(
        second_kernel,
        [jax.ShapeDtypeStruct((half, BLOCK, LANES), jnp.float32), block(2 * half + 1), edge, edge],
        came,
        "second",
        [pltpu.VMEM((2, half, BLOCK, LANES), jnp.float32)],
    )
    other = swap(send, 2)
    near = lax.ppermute(near, "gx", [(0, 1), (1, 0)])
    across = lax.ppermute(
        across, ("depth", "gx"), [(2 * i + g, 2 * (i ^ 2) + 1 - g) for i in range(bricks) for g in range(2)]
    )
    voxels = block(3, bricks)
    parts = call(
        functools.partial(staged_render_kernel, width, step_len),
        [block(4), voxels, voxels],
        [keep, other, tf_table],
        "render",
        [pltpu.VMEM((bricks, BLOCK, LANES), jnp.float32)],
        pl.CostEstimate(flops=1 << 24, bytes_accessed=1 << 23, transcendentals=0),
    )
    return call(
        functools.partial(staged_finish_kernel, width),
        jax.ShapeDtypeStruct((4, rows, width), jnp.float32),
        [*parts, across, near],
        "finish",
        [pltpu.VMEM((2, bricks, LANES), jnp.float32)],
    )


def body(density, tf_index, tf_table):
    bricks, ranks = lax.axis_size("depth"), lax.axis_size("gx")
    layers, rows, length = density.shape
    width = length // bricks
    if bricks == 16 and ranks == 2 and layers == 2 and rows == ROWS and 2 * width == LANES:
        return staged_body(density, tf_index, tf_table)
    assert layers == 2 and rows == ROWS and 2 * width <= LANES and LANES % width == 0
    step_len = 1.0 / (layers * bricks)
    edge = jax.ShapeDtypeStruct((2, bricks, LANES), jnp.float32)
    paired = ranks == 2
    inputs = [pltpu.with_memory_space_constraint(a, pltpu.HBM) for a in (density, tf_index)]
    landing = [
        pltpu.VMEM(density.shape, density.dtype),
        pltpu.VMEM(tf_index.shape, tf_index.dtype),
        pltpu.SemaphoreType.DMA,
        pltpu.SemaphoreType.DMA,
    ]
    packed = pl.pallas_call(
        functools.partial(pack_kernel, width),
        out_shape=jax.ShapeDtypeStruct((bricks, BLOCK, LANES), jnp.float32),
        in_specs=[pl.BlockSpec(memory_space=pltpu.HBM)] * 2,
        out_specs=WHOLE,
        scratch_shapes=landing,
        name="pack",
        compiler_params=PARAMS,
    )(*inputs)
    got = lax.all_to_all(packed, "depth", 0, 0, tiled=True)
    outer = pl.pallas_call(
        edge_pick_kernel if paired else edge_kernel,
        out_shape=[edge] * (1 if paired else 2),
        in_specs=[WHOLE],
        out_specs=[WHOLE] * (1 if paired else 2),
        name="edge",
        compiler_params=PARAMS,
    )(got)
    if paired:
        edges = [lax.ppermute(outer[0], "gx", [(0, 1), (1, 0)])]
    else:
        edges = [
            lax.ppermute(outer[1], "gx", [(i, i + 1) for i in range(ranks - 1)]),
            lax.ppermute(outer[0], "gx", [(i + 1, i) for i in range(ranks - 1)]),
        ]
    voxels = jax.ShapeDtypeStruct((3, bricks, ROWS, LANES), jnp.float32)
    parts = pl.pallas_call(
        functools.partial(render_kernel, width, step_len),
        out_shape=[jax.ShapeDtypeStruct((4, ROWS, LANES), jnp.float32), voxels, voxels],
        in_specs=[WHOLE] * 2,
        out_specs=[WHOLE] * 3,
        cost_estimate=pl.CostEstimate(flops=1 << 24, bytes_accessed=1 << 23, transcendentals=0),
        name="render",
        compiler_params=PARAMS,
    )(got, tf_table)
    return pl.pallas_call(
        functools.partial(finish_kernel, width, paired),
        out_shape=jax.ShapeDtypeStruct((4, rows, width), jnp.float32),
        in_specs=[WHOLE] * (3 + len(edges)),
        out_specs=WHOLE,
        name="finish",
        compiler_params=PARAMS,
    )(*parts, *edges)


def solution(mesh):
    in_specs = (P("depth", "gx", None), P("depth", "gx", None), P())
    out_specs = P(None, "gx", "depth")
    return jax.shard_map(body, mesh=mesh, in_specs=in_specs, out_specs=out_specs, check_vma=False)
```

```python
import functools

import jax
import jax.numpy as jnp
from jax import lax
from jax.experimental import pallas as pl
from jax.experimental.pallas import tpu as pltpu
from jax.sharding import PartitionSpec as P

LANES = 128
ROWS = 8
BLOCK = 3 * ROWS
FAR = (((2, 3, 1, 0), (1, 2, 3, 0)), ((3, 2, 0, 1), (2, 3, 0, 1)), ((1, 0, 3, 2), (3, 0, 1, 2)), ((0, 1, 2, 3), (0, 1, 2, 3)))
WHOLE = pl.BlockSpec(memory_space=pltpu.VMEM)
PARAMS = pltpu.CompilerParams(vmem_limit_bytes=4 << 20)


def pack_kernel(width, dens_hbm, index_hbm, out_ref, dens_ref, index_ref, dens_sem, index_sem):
    dens_copy = pltpu.make_async_copy(dens_hbm, dens_ref, dens_sem)
    index_copy = pltpu.make_async_copy(index_hbm, index_ref, index_sem)
    dens_copy.start()
    index_copy.start()
    dens_copy.wait()
    index_copy.wait()
    length = dens_ref.shape[2]
    lane = lax.broadcasted_iota(jnp.int32, (ROWS, LANES), 1)
    column = lax.broadcasted_iota(jnp.int32, (ROWS, length), 1)
    dens = [dens_ref[0], dens_ref[1]]
    index = [index_ref[0].astype(jnp.float32), index_ref[1].astype(jnp.float32)]
    before = [jnp.where(column == 0, 0.0, pltpu.roll(d, 1, 1)) for d in dens]
    after = [jnp.where(column == length - 1, 0.0, pltpu.roll(d, length - 1, 1)) for d in dens]

    def block(pair, j):
        start = (width * j) // LANES * LANES
        shift = width * j - start
        layers = []
        for layer, value in enumerate(pair):
            amount = (layer * width - shift) % LANES
            window = value[:, start : start + LANES]
            layers.append(pltpu.roll(window, amount, 1) if amount else window)
        return jnp.where(lane < width, layers[0], layers[1])

    for j in range(length // width):
        out_ref[j, 0:ROWS] = block(dens, j)
        out_ref[j, ROWS : 2 * ROWS] = block(index, j)
        out_ref[j, 2 * ROWS : 3 * ROWS] = jnp.where(
            lane % width == 0, block(before, j), block(after, j)
        )


def entry(tables, rank, core):
    value = tables[0][0]
    for c, table in enumerate(tables):
        for place, item in enumerate(table):
            if (c, place) != (0, 0):
                value = jnp.where((rank == place) & (core == c), item, value)
    return value


def origins(tables):
    return tuple(tuple(table.index(place) for place in range(len(table))) for table in tables)


def load_kernel(dens_hbm, index_hbm, dens_ref, index_ref, dens_sem, index_sem):
    dens_copy = pltpu.make_async_copy(dens_hbm, dens_ref, dens_sem)
    index_copy = pltpu.make_async_copy(index_hbm, index_ref, index_sem)
    dens_copy.start()
    index_copy.start()
    dens_copy.wait()
    index_copy.wait()


def first_kernel(*refs):
    own, other, outs, scratch = refs[0:2], refs[2:4], refs[4:-1], refs[-1]
    half = LANES // 2
    mine = lax.axis_index("depth")
    core = mine % 2
    lane = lax.broadcasted_iota(jnp.int32, (ROWS, LANES), 1)
    zero = jnp.zeros((ROWS, LANES), jnp.float32)
    tiles = own[0].shape[2] // LANES
    sides = [zero] * (tiles // 2)

    def tile_of(ref, layer, m):
        return ref[layer, :, m * LANES : (m + 1) * LANES] if 0 <= m < tiles else zero

    def pair(values):
        first = pltpu.roll(values[0], half * core, 1)
        return jnp.where(lane < half, first, pltpu.roll(values[1], half * (1 - core), 1))

    for n, (dens_ref, index_ref) in enumerate((own, other)):
        slot = core ^ n
        for m in range(tiles):
            group, place = divmod(m, 2)
            scratch[group, 4 * place + slot] = pair([tile_of(dens_ref, layer, m) for layer in range(2)])
            scratch[group, 4 * place + 2 + slot] = pair(
                [tile_of(index_ref, layer, m).astype(jnp.float32) for layer in range(2)]
            )
            brick = 2 * place + slot
            for layer in range(2):
                here = tile_of(dens_ref, layer, m)
                before = jnp.where(core == 0, tile_of(dens_ref, layer, m - 1), here)
                after = jnp.where(core == 0, here, tile_of(dens_ref, layer, m + 1))
                at = half * layer + brick
                moved = pltpu.roll(before, (at + 1 + half * core) % LANES, 1)
                sides[group] = jnp.where(lane == at, moved, sides[group])
                at = half * layer + half - 1 - brick
                moved = pltpu.roll(after, (at + half + half * core) % LANES, 1)
                sides[group] = jnp.where(lane == at, moved, sides[group])
    for group, side in enumerate(sides):
        scratch[group, ROWS] = side
    for step, out_ref in zip(FAR, outs):
        out_ref[...] = scratch[entry(step, mine // 4, core)]


def second_kernel(*refs):
    pieces, (keep_ref, send_ref, near_ref, across_ref, scratch) = refs[: len(FAR)], refs[len(FAR) :]
    half = LANES // 2
    mine = lax.axis_index("depth")
    place = mine // 2 % 2
    lane = lax.broadcasted_iota(jnp.int32, (ROWS, LANES), 1)
    for step, piece in zip(FAR, pieces):
        group = entry(origins(step), mine // 4, mine % 2)
        packed = piece[ROWS]
        for x in range(2):
            for core in range(2):
                brick = 2 * group + core
                p = 2 * x + core
                first = pltpu.roll(packed, LANES - p, 1) if p else packed
                last = pltpu.roll(packed, p, 1) if p else packed
                scratch[x, brick, 0:ROWS] = piece[4 * x + core]
                scratch[x, brick, ROWS : 2 * ROWS] = piece[4 * x + 2 + core]
                scratch[x, brick, 2 * ROWS :] = jnp.where(lane % half == 0, first, last)
    bricks = scratch.shape[1]
    sides = jnp.zeros((ROWS, LANES), jnp.float32)
    for brick in range(bricks):
        keep_ref[brick] = scratch[place, brick]
        send_ref[brick] = scratch[1 - place, brick, 0:ROWS]
        send_ref[bricks + brick] = scratch[1 - place, brick, ROWS : 2 * ROWS]
        side = scratch[1 - place, brick, 2 * ROWS :]
        first = pltpu.roll(side, brick, 1) if brick else side
        last = pltpu.roll(side, LANES - brick, 1) if brick else side
        sides = jnp.where(lane % half == brick, first, sides)
        sides = jnp.where(lane % half == half - 1 - brick, last, sides)
    send_ref[2 * bricks] = sides
    top = lax.axis_index("gx") == 0
    for ref, x in ((near_ref, place), (across_ref, 1 - place)):
        for part in range(2):
            low = 2 * ROWS * part
            ref[part] = jnp.where(top, scratch[x, :, low + ROWS - 1, :], scratch[x, :, low, :])


def staged_render_kernel(width, step_len, keep_ref, came_ref, table_ref, *refs):
    outs, got_ref = refs[:-1], refs[-1]
    half = LANES // 2
    place = lax.axis_index("depth") // 2 % 2
    lane = lax.broadcasted_iota(jnp.int32, (ROWS, LANES), 1)
    bricks = keep_ref.shape[0]
    packed = came_ref[2 * bricks]
    for brick in range(bricks):
        group, core = divmod(brick, 2)
        got_ref[4 * group + 2 * place + core] = keep_ref[brick]
        target = 4 * group + 2 * (1 - place) + core
        first = pltpu.roll(packed, LANES - brick, 1) if brick else packed
        last = pltpu.roll(packed, brick, 1) if brick else packed
        got_ref[target, 0:ROWS] = came_ref[brick]
        got_ref[target, ROWS : 2 * ROWS] = came_ref[bricks + brick]
        got_ref[target, 2 * ROWS :] = jnp.where(lane % half == 0, first, last)
    render_kernel(width, step_len, got_ref, table_ref, *outs)


def staged_finish_kernel(width, image_ref, grad_ref, weight_ref, across_ref, near_ref, out_ref, edge_ref):
    place = lax.axis_index("depth") // 2 % 2
    for part in range(2):
        near, across = near_ref[part], across_ref[part]
        for x, value in enumerate((jnp.where(place == 0, near, across), jnp.where(place == 0, across, near))):
            for group in range(len(FAR)):
                start = 4 * group + 2 * x
                edge_ref[part, start : start + 2] = value[2 * group : 2 * group + 2]
    finish_kernel(width, True, image_ref, grad_ref, weight_ref, edge_ref, out_ref)


def edge_kernel(got_ref, low_ref, high_ref):
    low_ref[0] = got_ref[:, 0, :]
    low_ref[1] = got_ref[:, 2 * ROWS, :]
    high_ref[0] = got_ref[:, ROWS - 1, :]
    high_ref[1] = got_ref[:, 3 * ROWS - 1, :]


def edge_pick_kernel(got_ref, edge_ref):
    first = lax.axis_index("gx") == 0
    edge_ref[0] = jnp.where(first, got_ref[:, ROWS - 1, :], got_ref[:, 0, :])
    edge_ref[1] = jnp.where(first, got_ref[:, 3 * ROWS - 1, :], got_ref[:, 2 * ROWS, :])


def trade(value, lane, width):
    if 2 * width == LANES:
        return pltpu.roll(value, width, 1)
    return jnp.where(lane < width, pltpu.roll(value, LANES - width, 1), pltpu.roll(value, width, 1))


def gather_rows(parts, index):
    within = index & (LANES - 1)
    value = jnp.take_along_axis(parts[0], within, axis=1, mode="promise_in_bounds")
    for k in range(1, len(parts)):
        more = jnp.take_along_axis(parts[k], within, axis=1, mode="promise_in_bounds")
        value = jnp.where(index >= k * LANES, more, value)
    return value


def lighting(grad_z, grad_x, grad_y):
    inverse = lax.rsqrt(grad_z * grad_z + grad_x * grad_x + grad_y * grad_y + 1.0)
    ndl = (0.48 * grad_z + 0.6 * grad_x + 0.64 * grad_y) * inverse
    ndh = (0.86023 * grad_z + 0.34875 * grad_x + 0.372 * grad_y) * inverse
    shine = jnp.maximum(ndh, 0.0)
    shine = shine * shine
    shine = shine * shine
    shine = shine * shine
    return 0.3 + 0.6 * jnp.abs(ndl) + 0.4 * shine


def along_y(inner, outer, width):
    lane = lax.broadcasted_iota(jnp.int32, inner.shape, 1)
    before = jnp.where(lane % width == 0, outer, pltpu.roll(inner, 1, 1))
    after = jnp.where(lane % width == width - 1, outer, pltpu.roll(inner, LANES - 1, 1))
    return before, after


def render_kernel(width, step_len, got_ref, table_ref, image_ref, grad_ref, weight_ref):
    bricks = got_ref.shape[0]
    levels = table_ref.shape[1]
    lane = lax.broadcasted_iota(jnp.int32, (ROWS, LANES), 1)
    row = lax.broadcasted_iota(jnp.int32, (ROWS, LANES), 0)
    front_layer = lane < width
    zero = jnp.zeros((ROWS, LANES), jnp.float32)
    table = [
        [
            jnp.broadcast_to(table_ref[c : c + 1, start : start + LANES], (ROWS, LANES))
            for start in range(0, levels, LANES)
        ]
        for c in range(4)
    ]

    def with_ends(values):
        return [zero] + [trade(value, lane, width) for value in values] + [zero]

    dens = [got_ref[k, 0:ROWS] for k in range(bricks)]
    side = [got_ref[k, 2 * ROWS : 3 * ROWS] for k in range(bricks)]
    dens_other, side_other = with_ends(dens), with_ends(side)

    def stencil(value, other, k):
        behind = jnp.where(front_layer, other[k + 1], other[k + 2])
        ahead = jnp.where(front_layer, other[k], other[k + 1])
        planes = (behind - ahead, ahead + 2.0 * value + behind)
        below = [jnp.where(row == 0, 0.0, pltpu.roll(plane, 1, 0)) for plane in planes]
        above = [jnp.where(row == ROWS - 1, 0.0, pltpu.roll(plane, ROWS - 1, 0)) for plane in planes]
        return (
            below[0] + 2.0 * planes[0] + above[0],
            above[1] - below[1],
            below[1] + 2.0 * planes[1] + above[1],
        )

    front = jnp.ones((ROWS, LANES), jnp.float32)
    image = [zero, zero, zero]
    for k in range(bricks):
        inner = stencil(dens[k], dens_other, k)
        outer = stencil(side[k], side_other, k)
        before, after = along_y(inner[0], outer[0], width)
        grad_z = (before + 2.0 * inner[0] + after) * 0.5
        before, after = along_y(inner[1], outer[1], width)
        grad_x = (before + 2.0 * inner[1] + after) * 0.5
        before, after = along_y(inner[2], outer[2], width)
        grad_y = (after - before) * 0.5
        lit = lighting(grad_z, grad_x, grad_y)

        index = got_ref[k, ROWS : 2 * ROWS].astype(jnp.int32)
        alpha = 1.0 - jnp.exp(-gather_rows(table[3], index) * dens[k] * step_len)
        transmit = 1.0 - alpha
        transmit_other = trade(transmit, lane, width)
        seen = jnp.where(front_layer, front, front * transmit_other) * alpha
        front = front * (transmit * transmit_other)
        for part, grad in enumerate((grad_z, grad_x, grad_y)):
            grad_ref[part, k] = grad
        for c in range(3):
            weight = seen * gather_rows(table[c], index)
            weight_ref[c, k] = weight
            image[c] = image[c] + weight * lit

    for c in range(3):
        image_ref[c] = image[c] + trade(image[c], lane, width)
    image_ref[3] = 1.0 - front


def finish_kernel(width, paired, image_ref, grad_ref, weight_ref, *refs):
    edge_refs, out_ref = refs[:-1], refs[-1]
    bricks = grad_ref.shape[1]
    brick = lax.broadcasted_iota(jnp.int32, (bricks, LANES), 0)
    lane = lax.broadcasted_iota(jnp.int32, (bricks, LANES), 1)

    def planes(values):
        other = trade(values, lane, width)
        later = jnp.where(brick == bricks - 1, 0.0, pltpu.roll(other, bricks - 1, 0))
        earlier = jnp.where(brick == 0, 0.0, pltpu.roll(other, 1, 0))
        behind = jnp.where(lane < width, other, later)
        ahead = jnp.where(lane < width, earlier, other)
        return (behind - ahead, ahead + 2.0 * values + behind)

    def outermost(edge_ref, grads, weights, sign):
        delta, total = planes(edge_ref[0])
        delta_side, total_side = planes(edge_ref[1])
        before, after = along_y(delta, delta_side, width)
        grad_z = grads[0] + (before + 2.0 * delta + after) * 0.5
        before, after = along_y(total, total_side, width)
        grad_x = grads[1] + sign * ((before + 2.0 * total + after) * 0.5)
        grad_y = grads[2] + (after - before) * 0.5
        lit = lighting(grad_z, grad_x, grad_y)
        sums = [jnp.sum(weight * lit, axis=0, keepdims=True) for weight in weights]
        return [total + trade(total, lane[:1], width) for total in sums]

    def row_of(ref, row):
        return [ref[part, :, row, :] for part in range(3)]

    row = lax.broadcasted_iota(jnp.int32, (ROWS, width), 0)
    image = [image_ref[c][:, :width] for c in range(3)]
    if paired:
        first = lax.axis_index("gx") == 0
        pick = lambda ref: [
            jnp.where(first, high, low) for high, low in zip(row_of(ref, ROWS - 1), row_of(ref, 0))
        ]
        sign = jnp.where(first, 1.0, -1.0)
        done = outermost(edge_refs[0], pick(grad_ref), pick(weight_ref), sign)
        place = jnp.where(first, ROWS - 1, 0)
        for c in range(3):
            out_ref[c] = jnp.where(row == place, done[c][:, :width], image[c])
    else:
        low = outermost(edge_refs[0], row_of(grad_ref, 0), row_of(weight_ref, 0), -1.0)
        last = ROWS - 1
        high = outermost(edge_refs[1], row_of(grad_ref, last), row_of(weight_ref, last), 1.0)
        for c in range(3):
            value = jnp.where(row == 0, low[c][:, :width], image[c])
            out_ref[c] = jnp.where(row == last, high[c][:, :width], value)
    out_ref[3] = image_ref[3][:, :width]


def staged_body(density, tf_index, tf_table):
    bricks, groups = lax.axis_size("depth"), len(FAR)
    layers, rows, length = density.shape
    width = length // bricks
    step_len = 1.0 / (layers * bricks)
    half = bricks // 2

    def call(kernel, out_shape, operands, name, scratch=(), cost=None, spec=WHOLE):
        return pl.pallas_call(
            kernel,
            out_shape=out_shape,
            in_specs=[spec] * len(operands),
            out_specs=jax.tree.map(lambda _: WHOLE, out_shape),
            scratch_shapes=scratch,
            cost_estimate=cost,
            name=name,
            compiler_params=PARAMS,
        )(*operands)

    def block(*shape):
        return jax.ShapeDtypeStruct(shape + (ROWS, LANES), jnp.float32)

    def swap(value, mask):
        return lax.ppermute(value, "depth", [(i, i ^ mask) for i in range(bricks)])

    inputs = [pltpu.with_memory_space_constraint(a, pltpu.HBM) for a in (density, tf_index)]
    theirs = [swap(value, 1) for value in (density, tf_index)]
    ours = call(
        load_kernel,
        [jax.ShapeDtypeStruct(a.shape, a.dtype) for a in inputs],
        inputs,
        "load",
        [pltpu.SemaphoreType.DMA] * 2,
        pl.CostEstimate(flops=1 << 20, bytes_accessed=1 << 21, transcendentals=0),
        pl.BlockSpec(memory_space=pltpu.HBM),
    )
    sent = call(
        first_kernel,
        [block(ROWS + 1)] * groups,
        [*ours, *theirs],
        "first",
        [pltpu.VMEM((groups, ROWS + 1, ROWS, LANES), jnp.float32)],
    )
    came = []
    for value, step in zip(sent, FAR):
        pairs = [(i, step[i % 2][i // 4] * 4 + i % 4) for i in range(bricks)]
        came.append(lax.ppermute(value, "depth", pairs) if step != FAR[-1] else value)
    edge = jax.ShapeDtypeStruct((2, half, LANES), jnp.float32)
    keep, send, near, across = call(
        second_kernel,
        [jax.ShapeDtypeStruct((half, BLOCK, LANES), jnp.float32), block(2 * half + 1), edge, edge],
        came,
        "second",
        [pltpu.VMEM((2, half, BLOCK, LANES), jnp.float32)],
    )
    other = swap(send, 2)
    near = lax.ppermute(near, "gx", [(0, 1), (1, 0)])
    across = lax.ppermute(
        across, ("depth", "gx"), [(2 * i + g, 2 * (i ^ 2) + 1 - g) for i in range(bricks) for g in range(2)]
    )
    voxels = block(3, bricks)
    parts = call(
        functools.partial(staged_render_kernel, width, step_len),
        [block(4), voxels, voxels],
        [keep, other, tf_table],
        "render",
        [pltpu.VMEM((bricks, BLOCK, LANES), jnp.float32)],
        pl.CostEstimate(flops=1 << 24, bytes_accessed=1 << 23, transcendentals=0),
    )
    return call(
        functools.partial(staged_finish_kernel, width),
        jax.ShapeDtypeStruct((4, rows, width), jnp.float32),
        [*parts, across, near],
        "finish",
        [pltpu.VMEM((2, bricks, LANES), jnp.float32)],
    )


def body(density, tf_index, tf_table):
    bricks, ranks = lax.axis_size("depth"), lax.axis_size("gx")
    layers, rows, length = density.shape
    width = length // bricks
    if bricks == 16 and ranks == 2 and layers == 2 and rows == ROWS and 2 * width == LANES:
        return staged_body(density, tf_index, tf_table)
    assert layers == 2 and rows == ROWS and 2 * width <= LANES and LANES % width == 0
    step_len = 1.0 / (layers * bricks)
    edge = jax.ShapeDtypeStruct((2, bricks, LANES), jnp.float32)
    paired = ranks == 2
    inputs = [pltpu.with_memory_space_constraint(a, pltpu.HBM) for a in (density, tf_index)]
    landing = [
        pltpu.VMEM(density.shape, density.dtype),
        pltpu.VMEM(tf_index.shape, tf_index.dtype),
        pltpu.SemaphoreType.DMA,
        pltpu.SemaphoreType.DMA,
    ]
    packed = pl.pallas_call(
        functools.partial(pack_kernel, width),
        out_shape=jax.ShapeDtypeStruct((bricks, BLOCK, LANES), jnp.float32),
        in_specs=[pl.BlockSpec(memory_space=pltpu.HBM)] * 2,
        out_specs=WHOLE,
        scratch_shapes=landing,
        name="pack",
        compiler_params=PARAMS,
    )(*inputs)
    got = lax.all_to_all(packed, "depth", 0, 0, tiled=True)
    outer = pl.pallas_call(
        edge_pick_kernel if paired else edge_kernel,
        out_shape=[edge] * (1 if paired else 2),
        in_specs=[WHOLE],
        out_specs=[WHOLE] * (1 if paired else 2),
        name="edge",
        compiler_params=PARAMS,
    )(got)
    if paired:
        edges = [lax.ppermute(outer[0], "gx", [(0, 1), (1, 0)])]
    else:
        edges = [
            lax.ppermute(outer[1], "gx", [(i, i + 1) for i in range(ranks - 1)]),
            lax.ppermute(outer[0], "gx", [(i + 1, i) for i in range(ranks - 1)]),
        ]
    voxels = jax.ShapeDtypeStruct((3, bricks, ROWS, LANES), jnp.float32)
    parts = pl.pallas_call(
        functools.partial(render_kernel, width, step_len),
        out_shape=[jax.ShapeDtypeStruct((4, ROWS, LANES), jnp.float32), voxels, voxels],
        in_specs=[WHOLE] * 2,
        out_specs=[WHOLE] * 3,
        cost_estimate=pl.CostEstimate(flops=1 << 24, bytes_accessed=1 << 23, transcendentals=0),
        name="render",
        compiler_params=PARAMS,
    )(got, tf_table)
    return pl.pallas_call(
        functools.partial(finish_kernel, width, paired),
        out_shape=jax.ShapeDtypeStruct((4, rows, width), jnp.float32),
        in_specs=[WHOLE] * (3 + len(edges)),
        out_specs=WHOLE,
        name="finish",
        compiler_params=PARAMS,
    )(*parts, *edges)


def solution(mesh):
    in_specs = (P("depth", "gx", None), P("depth", "gx", None), P())
    out_specs = P(None, "gx", "depth")
    return jax.shard_map(body, mesh=mesh, in_specs=in_specs, out_specs=out_specs, check_vma=False)
```

```python
import functools

import jax
import jax.numpy as jnp
from jax import lax
from jax.experimental import pallas as pl
from jax.experimental.pallas import tpu as pltpu
from jax.sharding import PartitionSpec as P


LANES = 128
ROWS = 8
BLOCK = 3 * ROWS
FAR = (((2, 3, 1, 0), (1, 2, 3, 0)), ((3, 2, 0, 1), (2, 3, 0, 1)), ((1, 0, 3, 2), (3, 0, 1, 2)), ((0, 1, 2, 3), (0, 1, 2, 3)))
WHOLE = pl.BlockSpec(memory_space=pltpu.VMEM)
PARAMS = pltpu.CompilerParams(vmem_limit_bytes=4 << 20)


def pack_kernel(width, dens_hbm, index_hbm, out_ref, dens_ref, index_ref, dens_sem, index_sem):
    dens_copy = pltpu.make_async_copy(dens_hbm, dens_ref, dens_sem)
    index_copy = pltpu.make_async_copy(index_hbm, index_ref, index_sem)
    dens_copy.start()
    index_copy.start()
    dens_copy.wait()
    index_copy.wait()
    length = dens_ref.shape[2]
    lane = lax.broadcasted_iota(jnp.int32, (ROWS, LANES), 1)
    column = lax.broadcasted_iota(jnp.int32, (ROWS, length), 1)
    dens = [dens_ref[0], dens_ref[1]]
    index = [index_ref[0].astype(jnp.float32), index_ref[1].astype(jnp.float32)]
    before = [jnp.where(column == 0, 0.0, pltpu.roll(d, 1, 1)) for d in dens]
    after = [jnp.where(column == length - 1, 0.0, pltpu.roll(d, length - 1, 1)) for d in dens]

    def block(pair, j):
        start = (width * j) // LANES * LANES
        shift = width * j - start
        layers = []
        for layer, value in enumerate(pair):
            amount = (layer * width - shift) % LANES
            window = value[:, start : start + LANES]
            layers.append(pltpu.roll(window, amount, 1) if amount else window)
        return jnp.where(lane < width, layers[0], layers[1])

    for j in range(length // width):
        out_ref[j, 0:ROWS] = block(dens, j)
        out_ref[j, ROWS : 2 * ROWS] = block(index, j)
        out_ref[j, 2 * ROWS : 3 * ROWS] = jnp.where(
            lane % width == 0, block(before, j), block(after, j)
        )


def entry(tables, rank, core):
    value = tables[0][0]
    for c, table in enumerate(tables):
        for place, item in enumerate(table):
            if (c, place) != (0, 0):
                value = jnp.where((rank == place) & (core == c), item, value)
    return value


def origins(tables):
    return tuple(tuple(table.index(place) for place in range(len(table))) for table in tables)


def load_kernel(dens_hbm, index_hbm, dens_ref, index_ref, dens_sem, index_sem):
    dens_copy = pltpu.make_async_copy(dens_hbm, dens_ref, dens_sem)
    index_copy = pltpu.make_async_copy(index_hbm, index_ref, index_sem)
    dens_copy.start()
    index_copy.start()
    dens_copy.wait()
    index_copy.wait()


def first_kernel(*refs):
    own, other, outs, scratch = refs[0:2], refs[2], refs[3:-1], refs[-1]
    half = LANES // 2
    mine = lax.axis_index("depth")
    core = mine % 2
    lane = lax.broadcasted_iota(jnp.int32, (ROWS, LANES), 1)
    zero = jnp.zeros((ROWS, LANES), jnp.float32)
    tiles = own[0].shape[2] // LANES
    sides = [zero] * (tiles // 2)

    def tile_of(ref, layer, m):
        return ref[layer, :, m * LANES : (m + 1) * LANES] if 0 <= m < tiles else zero

    def pair(values, core):
        first = pltpu.roll(values[0], half * core, 1)
        return jnp.where(lane < half, first, pltpu.roll(values[1], half * (1 - core), 1))

    for m in range(tiles):
        group, place = divmod(m, 2)
        index = [tile_of(own[1], layer, m).astype(jnp.float32) for layer in range(2)]
        scratch[group, 4 * place + 2] = jnp.where(lane < half, index[0], pltpu.roll(index[1], half, 1))
        scratch[group, 4 * place + 3] = jnp.where(lane < half, pltpu.roll(index[0], half, 1), index[1])

    for n, dens_ref in enumerate((own[0], other)):
        slot = core ^ n
        for m in range(tiles):
            group, place = divmod(m, 2)
            scratch[group, 4 * place + slot] = pair(
                [tile_of(dens_ref, layer, m) for layer in range(2)], core
            )
            brick = 2 * place + slot
            for layer in range(2):
                here = tile_of(dens_ref, layer, m)
                before = jnp.where(core == 0, tile_of(dens_ref, layer, m - 1), here)
                after = jnp.where(core == 0, here, tile_of(dens_ref, layer, m + 1))
                at = half * layer + brick
                moved = pltpu.roll(before, (at + 1 + half * core) % LANES, 1)
                sides[group] = jnp.where(lane == at, moved, sides[group])
                at = half * layer + half - 1 - brick
                moved = pltpu.roll(after, (at + half + half * core) % LANES, 1)
                sides[group] = jnp.where(lane == at, moved, sides[group])
    for group, side in enumerate(sides):
        scratch[group, ROWS] = side
    for step, out_ref in zip(FAR, outs):
        out_ref[...] = scratch[entry(step, mine // 4, core)]


def second_kernel(*refs):
    pieces, refs = refs[: len(FAR)], refs[len(FAR) :]
    keep_ref, index_ref, send_ref, near_ref, across_ref, scratch, index_scratch = refs
    half = LANES // 2
    mine = lax.axis_index("depth")
    place = mine // 2 % 2
    lane = lax.broadcasted_iota(jnp.int32, (ROWS, LANES), 1)
    for step, piece in zip(FAR, pieces):
        group = entry(origins(step), mine // 4, mine % 2)
        packed = piece[ROWS]
        for x in range(2):
            for core in range(2):
                brick = 2 * group + core
                p = 2 * x + core
                first = pltpu.roll(packed, LANES - p, 1) if p else packed
                last = pltpu.roll(packed, p, 1) if p else packed
                scratch[x, brick, 0:ROWS] = piece[4 * x + core]
                index_scratch[x, core, group] = piece[4 * x + 2 + core]
                scratch[x, brick, 2 * ROWS :] = jnp.where(lane % half == 0, first, last)
    bricks = scratch.shape[1]
    sides = jnp.zeros((ROWS, LANES), jnp.float32)
    for brick in range(bricks):
        keep_ref[brick] = scratch[place, brick]
        send_ref[brick] = scratch[1 - place, brick, 0:ROWS]
        index_ref[brick // 4, brick % 4] = index_scratch[place, brick // 4, brick % 4]
        send_ref[bricks + brick] = index_scratch[1 - place, brick // 4, brick % 4]
        side = scratch[1 - place, brick, 2 * ROWS :]
        first = pltpu.roll(side, brick, 1) if brick else side
        last = pltpu.roll(side, LANES - brick, 1) if brick else side
        sides = jnp.where(lane % half == brick, first, sides)
        sides = jnp.where(lane % half == half - 1 - brick, last, sides)
    send_ref[2 * bricks] = sides
    top = lax.axis_index("gx") == 0
    for ref, x in ((near_ref, place), (across_ref, 1 - place)):
        for part in range(2):
            low = 2 * ROWS * part
            ref[part] = jnp.where(top, scratch[x, :, low + ROWS - 1, :], scratch[x, :, low, :])


def index_kernel(index_ref, came_ref, out_ref):
    other = 1 - lax.axis_index("depth") % 2
    groups = index_ref.shape[1]
    for group in range(groups):
        out_ref[group] = index_ref[other, group]
        out_ref[groups + group] = came_ref[4 * groups // 2 + groups * other + group]


def staged_render_kernel(width, step_len, keep_ref, came_ref, index_ref, given_ref, table_ref, *refs):
    outs, got_ref = refs[:-1], refs[-1]
    half = LANES // 2
    place = lax.axis_index("depth") // 2 % 2
    lane = lax.broadcasted_iota(jnp.int32, (ROWS, LANES), 1)
    bricks = keep_ref.shape[0]
    packed = came_ref[2 * bricks]
    for brick in range(bricks):
        group, core = divmod(brick, 2)
        got_ref[4 * group + 2 * place + core] = keep_ref[brick]
        target = 4 * group + 2 * (1 - place) + core
        first = pltpu.roll(packed, LANES - brick, 1) if brick else packed
        last = pltpu.roll(packed, brick, 1) if brick else packed
        got_ref[target, 0:ROWS] = came_ref[brick]
        got_ref[target, 2 * ROWS :] = jnp.where(lane % half == 0, first, last)
    mine = lax.axis_index("depth") % 2
    for group in range(bricks // 2):
        for core, near, far in (
            (mine, index_ref[mine, group], came_ref[bricks + bricks // 2 * mine + group]),
            (1 - mine, given_ref[group], given_ref[bricks // 2 + group]),
        ):
            got_ref[4 * group + 2 * place + core, ROWS : 2 * ROWS] = near
            got_ref[4 * group + 2 * (1 - place) + core, ROWS : 2 * ROWS] = far
    render_kernel(width, step_len, got_ref, table_ref, *outs)


def staged_finish_kernel(width, image_ref, grad_ref, weight_ref, across_ref, near_ref, out_ref, edge_ref):
    place = lax.axis_index("depth") // 2 % 2
    for part in range(2):
        near, across = near_ref[part], across_ref[part]
        for x, value in enumerate((jnp.where(place == 0, near, across), jnp.where(place == 0, across, near))):
            for group in range(len(FAR)):
                start = 4 * group + 2 * x
                edge_ref[part, start : start + 2] = value[2 * group : 2 * group + 2]
    finish_kernel(width, True, image_ref, grad_ref, weight_ref, edge_ref, out_ref)


def edge_kernel(got_ref, low_ref, high_ref):
    low_ref[0] = got_ref[:, 0, :]
    low_ref[1] = got_ref[:, 2 * ROWS, :]
    high_ref[0] = got_ref[:, ROWS - 1, :]
    high_ref[1] = got_ref[:, 3 * ROWS - 1, :]


def edge_pick_kernel(got_ref, edge_ref):
    first = lax.axis_index("gx") == 0
    edge_ref[0] = jnp.where(first, got_ref[:, ROWS - 1, :], got_ref[:, 0, :])
    edge_ref[1] = jnp.where(first, got_ref[:, 3 * ROWS - 1, :], got_ref[:, 2 * ROWS, :])


def trade(value, lane, width):
    if 2 * width == LANES:
        return pltpu.roll(value, width, 1)
    return jnp.where(lane < width, pltpu.roll(value, LANES - width, 1), pltpu.roll(value, width, 1))


def gather_rows(parts, index):
    within = index & (LANES - 1)
    value = jnp.take_along_axis(parts[0], within, axis=1, mode="promise_in_bounds")
    for k in range(1, len(parts)):
        more = jnp.take_along_axis(parts[k], within, axis=1, mode="promise_in_bounds")
        value = jnp.where(index >= k * LANES, more, value)
    return value


def lighting(grad_z, grad_x, grad_y):
    inverse = lax.rsqrt(grad_z * grad_z + grad_x * grad_x + grad_y * grad_y + 1.0)
    ndl = (0.48 * grad_z + 0.6 * grad_x + 0.64 * grad_y) * inverse
    ndh = (0.86023 * grad_z + 0.34875 * grad_x + 0.372 * grad_y) * inverse
    shine = jnp.maximum(ndh, 0.0)
    shine = shine * shine
    shine = shine * shine
    shine = shine * shine
    return 0.3 + 0.6 * jnp.abs(ndl) + 0.4 * shine


def along_y(inner, outer, width):
    lane = lax.broadcasted_iota(jnp.int32, inner.shape, 1)
    before = jnp.where(lane % width == 0, outer, pltpu.roll(inner, 1, 1))
    after = jnp.where(lane % width == width - 1, outer, pltpu.roll(inner, LANES - 1, 1))
    return before, after


def render_kernel(width, step_len, got_ref, table_ref, image_ref, grad_ref, weight_ref):
    bricks = got_ref.shape[0]
    levels = table_ref.shape[1]
    lane = lax.broadcasted_iota(jnp.int32, (ROWS, LANES), 1)
    row = lax.broadcasted_iota(jnp.int32, (ROWS, LANES), 0)
    front_layer = lane < width
    zero = jnp.zeros((ROWS, LANES), jnp.float32)
    table = [
        [
            jnp.broadcast_to(table_ref[c : c + 1, start : start + LANES], (ROWS, LANES))
            for start in range(0, levels, LANES)
        ]
        for c in range(4)
    ]

    def with_ends(values):
        return [zero] + [trade(value, lane, width) for value in values] + [zero]

    dens = [got_ref[k, 0:ROWS] for k in range(bricks)]
    side = [got_ref[k, 2 * ROWS : 3 * ROWS] for k in range(bricks)]
    dens_other, side_other = with_ends(dens), with_ends(side)

    def stencil(value, other, k):
        behind = jnp.where(front_layer, other[k + 1], other[k + 2])
        ahead = jnp.where(front_layer, other[k], other[k + 1])
        planes = (behind - ahead, ahead + 2.0 * value + behind)
        below = [jnp.where(row == 0, 0.0, pltpu.roll(plane, 1, 0)) for plane in planes]
        above = [jnp.where(row == ROWS - 1, 0.0, pltpu.roll(plane, ROWS - 1, 0)) for plane in planes]
        return (
            below[0] + 2.0 * planes[0] + above[0],
            above[1] - below[1],
            below[1] + 2.0 * planes[1] + above[1],
        )

    front = jnp.ones((ROWS, LANES), jnp.float32)
    image = [zero, zero, zero]
    for k in range(bricks):
        inner = stencil(dens[k], dens_other, k)
        outer = stencil(side[k], side_other, k)
        before, after = along_y(inner[0], outer[0], width)
        grad_z = (before + 2.0 * inner[0] + after) * 0.5
        before, after = along_y(inner[1], outer[1], width)
        grad_x = (before + 2.0 * inner[1] + after) * 0.5
        before, after = along_y(inner[2], outer[2], width)
        grad_y = (after - before) * 0.5
        lit = lighting(grad_z, grad_x, grad_y)

        index = got_ref[k, ROWS : 2 * ROWS].astype(jnp.int32)
        alpha = 1.0 - jnp.exp(-gather_rows(table[3], index) * dens[k] * step_len)
        transmit = 1.0 - alpha
        transmit_other = trade(transmit, lane, width)
        seen = jnp.where(front_layer, front, front * transmit_other) * alpha
        front = front * (transmit * transmit_other)
        for part, grad in enumerate((grad_z, grad_x, grad_y)):
            grad_ref[part, k] = grad
        for c in range(3):
            weight = seen * gather_rows(table[c], index)
            weight_ref[c, k] = weight
            image[c] = image[c] + weight * lit

    for c in range(3):
        image_ref[c] = image[c] + trade(image[c], lane, width)
    image_ref[3] = 1.0 - front


def finish_kernel(width, paired, image_ref, grad_ref, weight_ref, *refs):
    edge_refs, out_ref = refs[:-1], refs[-1]
    bricks = grad_ref.shape[1]
    brick = lax.broadcasted_iota(jnp.int32, (bricks, LANES), 0)
    lane = lax.broadcasted_iota(jnp.int32, (bricks, LANES), 1)

    def planes(values):
        other = trade(values, lane, width)
        later = jnp.where(brick == bricks - 1, 0.0, pltpu.roll(other, bricks - 1, 0))
        earlier = jnp.where(brick == 0, 0.0, pltpu.roll(other, 1, 0))
        behind = jnp.where(lane < width, other, later)
        ahead = jnp.where(lane < width, earlier, other)
        return (behind - ahead, ahead + 2.0 * values + behind)

    def outermost(edge_ref, grads, weights, sign):
        delta, total = planes(edge_ref[0])
        delta_side, total_side = planes(edge_ref[1])
        before, after = along_y(delta, delta_side, width)
        grad_z = grads[0] + (before + 2.0 * delta + after) * 0.5
        before, after = along_y(total, total_side, width)
        grad_x = grads[1] + sign * ((before + 2.0 * total + after) * 0.5)
        grad_y = grads[2] + (after - before) * 0.5
        lit = lighting(grad_z, grad_x, grad_y)
        sums = [jnp.sum(weight * lit, axis=0, keepdims=True) for weight in weights]
        return [total + trade(total, lane[:1], width) for total in sums]

    def row_of(ref, row):
        return [ref[part, :, row, :] for part in range(3)]

    row = lax.broadcasted_iota(jnp.int32, (ROWS, width), 0)
    image = [image_ref[c][:, :width] for c in range(3)]
    if paired:
        first = lax.axis_index("gx") == 0
        pick = lambda ref: [
            jnp.where(first, high, low) for high, low in zip(row_of(ref, ROWS - 1), row_of(ref, 0))
        ]
        sign = jnp.where(first, 1.0, -1.0)
        done = outermost(edge_refs[0], pick(grad_ref), pick(weight_ref), sign)
        place = jnp.where(first, ROWS - 1, 0)
        for c in range(3):
            out_ref[c] = jnp.where(row == place, done[c][:, :width], image[c])
    else:
        low = outermost(edge_refs[0], row_of(grad_ref, 0), row_of(weight_ref, 0), -1.0)
        last = ROWS - 1
        high = outermost(edge_refs[1], row_of(grad_ref, last), row_of(weight_ref, last), 1.0)
        for c in range(3):
            value = jnp.where(row == 0, low[c][:, :width], image[c])
            out_ref[c] = jnp.where(row == last, high[c][:, :width], value)
    out_ref[3] = image_ref[3][:, :width]


def staged_body(density, tf_index, tf_table):
    bricks, groups = lax.axis_size("depth"), len(FAR)
    layers, rows, length = density.shape
    width = length // bricks
    step_len = 1.0 / (layers * bricks)
    half = bricks // 2

    def call(kernel, out_shape, operands, scratch=(), cost=None, spec=WHOLE):
        return pl.pallas_call(
            kernel,
            out_shape=out_shape,
            in_specs=[spec] * len(operands),
            out_specs=jax.tree.map(lambda _: WHOLE, out_shape),
            scratch_shapes=scratch,
            cost_estimate=cost,
            compiler_params=PARAMS,
        )(*operands)

    def block(*shape):
        return jax.ShapeDtypeStruct(shape + (ROWS, LANES), jnp.float32)

    def swap(value, mask):
        return lax.ppermute(value, "depth", [(i, i ^ mask) for i in range(bricks)])

    inputs = [pltpu.with_memory_space_constraint(a, pltpu.HBM) for a in (density, tf_index)]
    theirs = swap(density, 1)
    ours = call(
        load_kernel,
        [jax.ShapeDtypeStruct(a.shape, a.dtype) for a in inputs],
        inputs,
        [pltpu.SemaphoreType.DMA] * 2,
        pl.CostEstimate(flops=1 << 20, bytes_accessed=1 << 21, transcendentals=0),
        pl.BlockSpec(memory_space=pltpu.HBM),
    )
    sent = call(
        first_kernel,
        [block(ROWS + 1)] * groups,
        [*ours, theirs],
        [pltpu.VMEM((groups, ROWS + 1, ROWS, LANES), jnp.float32)],
    )
    came = []
    for value, step in zip(sent, FAR):
        pairs = [(i, step[i % 2][i // 4] * 4 + i % 4) for i in range(bricks)]
        came.append(lax.ppermute(value, "depth", pairs) if step != FAR[-1] else value)
    edge = jax.ShapeDtypeStruct((2, half, LANES), jnp.float32)
    keep, index, send, near, across = call(
        second_kernel,
        [jax.ShapeDtypeStruct((half, BLOCK, LANES), jnp.float32), block(2, groups), block(2 * half + 1), edge, edge],
        came,
        [
            pltpu.VMEM((2, half, BLOCK, LANES), jnp.float32),
            pltpu.VMEM((2, 2, groups, ROWS, LANES), jnp.float32),
        ],
    )
    other = swap(send, 2)
    near = lax.ppermute(near, "gx", [(0, 1), (1, 0)])
    across = lax.ppermute(
        across, ("depth", "gx"), [(2 * i + g, 2 * (i ^ 2) + 1 - g) for i in range(bricks) for g in range(2)]
    )
    given = call(index_kernel, block(half), [index, other])
    given = swap(given, 1)
    voxels = block(3, bricks)
    parts = call(
        functools.partial(staged_render_kernel, width, step_len),
        [block(4), voxels, voxels],
        [keep, other, index, given, tf_table],
        [pltpu.VMEM((bricks, BLOCK, LANES), jnp.float32)],
        pl.CostEstimate(flops=1 << 24, bytes_accessed=1 << 23, transcendentals=0),
    )
    return call(
        functools.partial(staged_finish_kernel, width),
        jax.ShapeDtypeStruct((4, rows, width), jnp.float32),
        [*parts, across, near],
        [pltpu.VMEM((2, bricks, LANES), jnp.float32)],
    )


def body(density, tf_index, tf_table):
    bricks, ranks = lax.axis_size("depth"), lax.axis_size("gx")
    layers, rows, length = density.shape
    width = length // bricks
    if bricks == 16 and ranks == 2 and layers == 2 and rows == ROWS and 2 * width == LANES:
        return staged_body(density, tf_index, tf_table)
    assert layers == 2 and rows == ROWS and 2 * width <= LANES and LANES % width == 0
    step_len = 1.0 / (layers * bricks)
    edge = jax.ShapeDtypeStruct((2, bricks, LANES), jnp.float32)
    paired = ranks == 2
    inputs = [pltpu.with_memory_space_constraint(a, pltpu.HBM) for a in (density, tf_index)]
    landing = [
        pltpu.VMEM(density.shape, density.dtype),
        pltpu.VMEM(tf_index.shape, tf_index.dtype),
        pltpu.SemaphoreType.DMA,
        pltpu.SemaphoreType.DMA,
    ]
    packed = pl.pallas_call(
        functools.partial(pack_kernel, width),
        out_shape=jax.ShapeDtypeStruct((bricks, BLOCK, LANES), jnp.float32),
        in_specs=[pl.BlockSpec(memory_space=pltpu.HBM)] * 2,
        out_specs=WHOLE,
        scratch_shapes=landing,
        name="pack",
        compiler_params=PARAMS,
    )(*inputs)
    got = lax.all_to_all(packed, "depth", 0, 0, tiled=True)
    outer = pl.pallas_call(
        edge_pick_kernel if paired else edge_kernel,
        out_shape=[edge] * (1 if paired else 2),
        in_specs=[WHOLE],
        out_specs=[WHOLE] * (1 if paired else 2),
        name="edge",
        compiler_params=PARAMS,
    )(got)
    if paired:
        edges = [lax.ppermute(outer[0], "gx", [(0, 1), (1, 0)])]
    else:
        edges = [
            lax.ppermute(outer[1], "gx", [(i, i + 1) for i in range(ranks - 1)]),
            lax.ppermute(outer[0], "gx", [(i + 1, i) for i in range(ranks - 1)]),
        ]
    voxels = jax.ShapeDtypeStruct((3, bricks, ROWS, LANES), jnp.float32)
    parts = pl.pallas_call(
        functools.partial(render_kernel, width, step_len),
        out_shape=[jax.ShapeDtypeStruct((4, ROWS, LANES), jnp.float32), voxels, voxels],
        in_specs=[WHOLE] * 2,
        out_specs=[WHOLE] * 3,
        cost_estimate=pl.CostEstimate(flops=1 << 24, bytes_accessed=1 << 23, transcendentals=0),
        name="render",
        compiler_params=PARAMS,
    )(got, tf_table)
    return pl.pallas_call(
        functools.partial(finish_kernel, width, paired),
        out_shape=jax.ShapeDtypeStruct((4, rows, width), jnp.float32),
        in_specs=[WHOLE] * (3 + len(edges)),
        out_specs=WHOLE,
        name="finish",
        compiler_params=PARAMS,
    )(*parts, *edges)


def solution(mesh):
    in_specs = (P("depth", "gx", None), P("depth", "gx", None), P())
    out_specs = P(None, "gx", "depth")
    return jax.shard_map(body, mesh=mesh, in_specs=in_specs, out_specs=out_specs, check_vma=False)
```

```python
import functools

import jax
import jax.numpy as jnp
from jax import lax
from jax.experimental import pallas as pl
from jax.experimental.pallas import tpu as pltpu
from jax.sharding import PartitionSpec as P


LANES = 128
ROWS = 8
BLOCK = 3 * ROWS
FAR = (((2, 3, 1, 0), (1, 2, 3, 0)), ((3, 2, 0, 1), (2, 3, 0, 1)), ((1, 0, 3, 2), (3, 0, 1, 2)), ((0, 1, 2, 3), (0, 1, 2, 3)))
WHOLE = pl.BlockSpec(memory_space=pltpu.VMEM)
PARAMS = pltpu.CompilerParams(vmem_limit_bytes=4 << 20)


def pack_kernel(width, dens_hbm, index_hbm, out_ref, dens_ref, index_ref, dens_sem, index_sem):
    dens_copy = pltpu.make_async_copy(dens_hbm, dens_ref, dens_sem)
    index_copy = pltpu.make_async_copy(index_hbm, index_ref, index_sem)
    dens_copy.start()
    index_copy.start()
    dens_copy.wait()
    index_copy.wait()
    length = dens_ref.shape[2]
    lane = lax.broadcasted_iota(jnp.int32, (ROWS, LANES), 1)
    column = lax.broadcasted_iota(jnp.int32, (ROWS, length), 1)
    dens = [dens_ref[0], dens_ref[1]]
    index = [index_ref[0].astype(jnp.float32), index_ref[1].astype(jnp.float32)]
    before = [jnp.where(column == 0, 0.0, pltpu.roll(d, 1, 1)) for d in dens]
    after = [jnp.where(column == length - 1, 0.0, pltpu.roll(d, length - 1, 1)) for d in dens]

    def block(pair, j):
        start = (width * j) // LANES * LANES
        shift = width * j - start
        layers = []
        for layer, value in enumerate(pair):
            amount = (layer * width - shift) % LANES
            window = value[:, start : start + LANES]
            layers.append(pltpu.roll(window, amount, 1) if amount else window)
        return jnp.where(lane < width, layers[0], layers[1])

    for j in range(length // width):
        out_ref[j, 0:ROWS] = block(dens, j)
        out_ref[j, ROWS : 2 * ROWS] = block(index, j)
        out_ref[j, 2 * ROWS : 3 * ROWS] = jnp.where(
            lane % width == 0, block(before, j), block(after, j)
        )


def entry(tables, rank, core):
    value = tables[0][0]
    for c, table in enumerate(tables):
        for place, item in enumerate(table):
            if (c, place) != (0, 0):
                value = jnp.where((rank == place) & (core == c), item, value)
    return value


def origins(tables):
    return tuple(tuple(table.index(place) for place in range(len(table))) for table in tables)


def tile_of(ref, layer, m):
    if 0 <= m < ref.shape[2] // LANES:
        return ref[layer, :, m * LANES : (m + 1) * LANES]
    return jnp.zeros((ROWS, LANES), jnp.float32)


def pair_of(ref, core, m):
    half = LANES // 2
    lane = lax.broadcasted_iota(jnp.int32, (ROWS, LANES), 1)
    first = pltpu.roll(tile_of(ref, 0, m), half * core, 1)
    return jnp.where(lane < half, first, pltpu.roll(tile_of(ref, 1, m), half * (1 - core), 1))


def add_sides(side, ref, core, m, brick):
    half = LANES // 2
    lane = lax.broadcasted_iota(jnp.int32, (ROWS, LANES), 1)
    for layer in range(2):
        here = tile_of(ref, layer, m)
        before = jnp.where(core == 0, tile_of(ref, layer, m - 1), here)
        after = jnp.where(core == 0, here, tile_of(ref, layer, m + 1))
        at = half * layer + brick
        side = jnp.where(lane == at, pltpu.roll(before, (at + 1 + half * core) % LANES, 1), side)
        at = half * layer + half - 1 - brick
        side = jnp.where(lane == at, pltpu.roll(after, (at + half + half * core) % LANES, 1), side)
    return side


def load_kernel(dens_hbm, index_hbm, part_ref, dens_ref, index_ref, dens_sem, index_sem):
    dens_copy = pltpu.make_async_copy(dens_hbm, dens_ref, dens_sem)
    index_copy = pltpu.make_async_copy(index_hbm, index_ref, index_sem)
    dens_copy.start()
    index_copy.start()
    core = lax.axis_index("depth") % 2
    half = LANES // 2
    lane = lax.broadcasted_iota(jnp.int32, (ROWS, LANES), 1)
    dens_copy.wait()
    for group in range(part_ref.shape[0]):
        side = jnp.zeros((ROWS, LANES), jnp.float32)
        for place in range(2):
            part_ref[group, place] = pair_of(dens_ref, core, 2 * group + place)
            side = add_sides(side, dens_ref, core, 2 * group + place, 2 * place + core)
        part_ref[group, 6] = side
    index_copy.wait()
    for group in range(part_ref.shape[0]):
        for place in range(2):
            first, second = (tile_of(index_ref, layer, 2 * group + place).astype(jnp.float32) for layer in range(2))
            part_ref[group, 2 + 2 * place] = jnp.where(lane < half, first, pltpu.roll(second, half, 1))
            part_ref[group, 3 + 2 * place] = jnp.where(lane < half, pltpu.roll(first, half, 1), second)


def first_kernel(part_ref, dens_ref, *refs):
    outs, scratch = refs[:-1], refs[-1]
    mine = lax.axis_index("depth")
    core = mine % 2
    for group in range(part_ref.shape[0]):
        side = part_ref[group, 6]
        for place in range(2):
            scratch[group, place] = pair_of(dens_ref, core, 2 * group + place)
            side = add_sides(side, dens_ref, core, 2 * group + place, 2 * place + 1 - core)
        scratch[group, 2] = side
    for step, out_ref in zip(FAR, outs):
        group = entry(step, mine // 4, core)
        for place in range(2):
            own, other = part_ref[group, place], scratch[group, place]
            out_ref[4 * place] = jnp.where(core == 0, own, other)
            out_ref[4 * place + 1] = jnp.where(core == 0, other, own)
            out_ref[4 * place + 2] = part_ref[group, 2 + 2 * place]
            out_ref[4 * place + 3] = part_ref[group, 3 + 2 * place]
        out_ref[ROWS] = scratch[group, 2]


def second_kernel(*refs):
    pieces, refs = refs[: len(FAR)], refs[len(FAR) :]
    keep_ref, index_ref, send_ref, near_ref, across_ref, scratch, index_scratch = refs
    half = LANES // 2
    mine = lax.axis_index("depth")
    place = mine // 2 % 2
    lane = lax.broadcasted_iota(jnp.int32, (ROWS, LANES), 1)
    for step, piece in zip(FAR, pieces):
        group = entry(origins(step), mine // 4, mine % 2)
        packed = piece[ROWS]
        for x in range(2):
            for core in range(2):
                brick = 2 * group + core
                p = 2 * x + core
                first = pltpu.roll(packed, LANES - p, 1) if p else packed
                last = pltpu.roll(packed, p, 1) if p else packed
                scratch[x, brick, 0:ROWS] = piece[4 * x + core]
                index_scratch[x, core, group] = piece[4 * x + 2 + core]
                scratch[x, brick, 2 * ROWS :] = jnp.where(lane % half == 0, first, last)
    bricks = scratch.shape[1]
    sides = jnp.zeros((ROWS, LANES), jnp.float32)
    for brick in range(bricks):
        keep_ref[brick] = scratch[place, brick]
        send_ref[brick] = scratch[1 - place, brick, 0:ROWS]
        index_ref[brick // 4, brick % 4] = index_scratch[place, brick // 4, brick % 4]
        send_ref[bricks + brick] = index_scratch[1 - place, brick // 4, brick % 4]
        side = scratch[1 - place, brick, 2 * ROWS :]
        first = pltpu.roll(side, brick, 1) if brick else side
        last = pltpu.roll(side, LANES - brick, 1) if brick else side
        sides = jnp.where(lane % half == brick, first, sides)
        sides = jnp.where(lane % half == half - 1 - brick, last, sides)
    send_ref[2 * bricks] = sides
    top = lax.axis_index("gx") == 0
    for ref, x in ((near_ref, place), (across_ref, 1 - place)):
        for part in range(2):
            low = 2 * ROWS * part
            ref[part] = jnp.where(top, scratch[x, :, low + ROWS - 1, :], scratch[x, :, low, :])


def index_kernel(index_ref, came_ref, out_ref):
    other = 1 - lax.axis_index("depth") % 2
    groups = index_ref.shape[1]
    for group in range(groups):
        out_ref[group] = index_ref[other, group]
        out_ref[groups + group] = came_ref[4 * groups // 2 + groups * other + group]


def staged_render_kernel(width, step_len, keep_ref, came_ref, index_ref, given_ref, table_ref, *refs):
    outs, got_ref = refs[:-1], refs[-1]
    half = LANES // 2
    place = lax.axis_index("depth") // 2 % 2
    lane = lax.broadcasted_iota(jnp.int32, (ROWS, LANES), 1)
    bricks = keep_ref.shape[0]
    packed = came_ref[2 * bricks]
    for brick in range(bricks):
        group, core = divmod(brick, 2)
        got_ref[4 * group + 2 * place + core] = keep_ref[brick]
        target = 4 * group + 2 * (1 - place) + core
        first = pltpu.roll(packed, LANES - brick, 1) if brick else packed
        last = pltpu.roll(packed, brick, 1) if brick else packed
        got_ref[target, 0:ROWS] = came_ref[brick]
        got_ref[target, 2 * ROWS :] = jnp.where(lane % half == 0, first, last)
    mine = lax.axis_index("depth") % 2
    for group in range(bricks // 2):
        for core, near, far in (
            (mine, index_ref[mine, group], came_ref[bricks + bricks // 2 * mine + group]),
            (1 - mine, given_ref[group], given_ref[bricks // 2 + group]),
        ):
            got_ref[4 * group + 2 * place + core, ROWS : 2 * ROWS] = near
            got_ref[4 * group + 2 * (1 - place) + core, ROWS : 2 * ROWS] = far
    render_kernel(width, step_len, got_ref, table_ref, *outs)


def staged_finish_kernel(width, image_ref, grad_ref, weight_ref, across_ref, near_ref, out_ref, edge_ref):
    place = lax.axis_index("depth") // 2 % 2
    for part in range(2):
        near, across = near_ref[part], across_ref[part]
        for x, value in enumerate((jnp.where(place == 0, near, across), jnp.where(place == 0, across, near))):
            for group in range(len(FAR)):
                start = 4 * group + 2 * x
                edge_ref[part, start : start + 2] = value[2 * group : 2 * group + 2]
    finish_kernel(width, True, image_ref, grad_ref, weight_ref, edge_ref, out_ref)


def edge_kernel(got_ref, low_ref, high_ref):
    low_ref[0] = got_ref[:, 0, :]
    low_ref[1] = got_ref[:, 2 * ROWS, :]
    high_ref[0] = got_ref[:, ROWS - 1, :]
    high_ref[1] = got_ref[:, 3 * ROWS - 1, :]


def edge_pick_kernel(got_ref, edge_ref):
    first = lax.axis_index("gx") == 0
    edge_ref[0] = jnp.where(first, got_ref[:, ROWS - 1, :], got_ref[:, 0, :])
    edge_ref[1] = jnp.where(first, got_ref[:, 3 * ROWS - 1, :], got_ref[:, 2 * ROWS, :])


def trade(value, lane, width):
    if 2 * width == LANES:
        return pltpu.roll(value, width, 1)
    return jnp.where(lane < width, pltpu.roll(value, LANES - width, 1), pltpu.roll(value, width, 1))


def gather_rows(parts, index):
    within = index & (LANES - 1)
    value = jnp.take_along_axis(parts[0], within, axis=1, mode="promise_in_bounds")
    for k in range(1, len(parts)):
        more = jnp.take_along_axis(parts[k], within, axis=1, mode="promise_in_bounds")
        value = jnp.where(index >= k * LANES, more, value)
    return value


def lighting(grad_z, grad_x, grad_y):
    inverse = lax.rsqrt(grad_z * grad_z + grad_x * grad_x + grad_y * grad_y + 1.0)
    ndl = (0.48 * grad_z + 0.6 * grad_x + 0.64 * grad_y) * inverse
    ndh = (0.86023 * grad_z + 0.34875 * grad_x + 0.372 * grad_y) * inverse
    shine = jnp.maximum(ndh, 0.0)
    shine = shine * shine
    shine = shine * shine
    shine = shine * shine
    return 0.3 + 0.6 * jnp.abs(ndl) + 0.4 * shine


def along_y(inner, outer, width):
    lane = lax.broadcasted_iota(jnp.int32, inner.shape, 1)
    before = jnp.where(lane % width == 0, outer, pltpu.roll(inner, 1, 1))
    after = jnp.where(lane % width == width - 1, outer, pltpu.roll(inner, LANES - 1, 1))
    return before, after


def render_kernel(width, step_len, got_ref, table_ref, image_ref, grad_ref, weight_ref):
    bricks = got_ref.shape[0]
    levels = table_ref.shape[1]
    lane = lax.broadcasted_iota(jnp.int32, (ROWS, LANES), 1)
    row = lax.broadcasted_iota(jnp.int32, (ROWS, LANES), 0)
    front_layer = lane < width
    zero = jnp.zeros((ROWS, LANES), jnp.float32)
    table = [
        [
            jnp.broadcast_to(table_ref[c : c + 1, start : start + LANES], (ROWS, LANES))
            for start in range(0, levels, LANES)
        ]
        for c in range(4)
    ]

    def with_ends(values):
        return [zero] + [trade(value, lane, width) for value in values] + [zero]

    dens = [got_ref[k, 0:ROWS] for k in range(bricks)]
    side = [got_ref[k, 2 * ROWS : 3 * ROWS] for k in range(bricks)]
    dens_other, side_other = with_ends(dens), with_ends(side)

    def stencil(value, other, k):
        behind = jnp.where(front_layer, other[k + 1], other[k + 2])
        ahead = jnp.where(front_layer, other[k], other[k + 1])
        planes = (behind - ahead, ahead + 2.0 * value + behind)
        below = [jnp.where(row == 0, 0.0, pltpu.roll(plane, 1, 0)) for plane in planes]
        above = [jnp.where(row == ROWS - 1, 0.0, pltpu.roll(plane, ROWS - 1, 0)) for plane in planes]
        return (
            below[0] + 2.0 * planes[0] + above[0],
            above[1] - below[1],
            below[1] + 2.0 * planes[1] + above[1],
        )

    front = jnp.ones((ROWS, LANES), jnp.float32)
    image = [zero, zero, zero]
    for k in range(bricks):
        inner = stencil(dens[k], dens_other, k)
        outer = stencil(side[k], side_other, k)
        before, after = along_y(inner[0], outer[0], width)
        grad_z = (before + 2.0 * inner[0] + after) * 0.5
        before, after = along_y(inner[1], outer[1], width)
        grad_x = (before + 2.0 * inner[1] + after) * 0.5
        before, after = along_y(inner[2], outer[2], width)
        grad_y = (after - before) * 0.5
        lit = lighting(grad_z, grad_x, grad_y)

        index = got_ref[k, ROWS : 2 * ROWS].astype(jnp.int32)
        alpha = 1.0 - jnp.exp(-gather_rows(table[3], index) * dens[k] * step_len)
        transmit = 1.0 - alpha
        transmit_other = trade(transmit, lane, width)
        seen = jnp.where(front_layer, front, front * transmit_other) * alpha
        front = front * (transmit * transmit_other)
        for part, grad in enumerate((grad_z, grad_x, grad_y)):
            grad_ref[part, k] = grad
        for c in range(3):
            weight = seen * gather_rows(table[c], index)
            weight_ref[c, k] = weight
            image[c] = image[c] + weight * lit

    for c in range(3):
        image_ref[c] = image[c] + trade(image[c], lane, width)
    image_ref[3] = 1.0 - front


def finish_kernel(width, paired, image_ref, grad_ref, weight_ref, *refs):
    edge_refs, out_ref = refs[:-1], refs[-1]
    bricks = grad_ref.shape[1]
    brick = lax.broadcasted_iota(jnp.int32, (bricks, LANES), 0)
    lane = lax.broadcasted_iota(jnp.int32, (bricks, LANES), 1)

    def planes(values):
        other = trade(values, lane, width)
        later = jnp.where(brick == bricks - 1, 0.0, pltpu.roll(other, bricks - 1, 0))
        earlier = jnp.where(brick == 0, 0.0, pltpu.roll(other, 1, 0))
        behind = jnp.where(lane < width, other, later)
        ahead = jnp.where(lane < width, earlier, other)
        return (behind - ahead, ahead + 2.0 * values + behind)

    def outermost(edge_ref, grads, weights, sign):
        delta, total = planes(edge_ref[0])
        delta_side, total_side = planes(edge_ref[1])
        before, after = along_y(delta, delta_side, width)
        grad_z = grads[0] + (before + 2.0 * delta + after) * 0.5
        before, after = along_y(total, total_side, width)
        grad_x = grads[1] + sign * ((before + 2.0 * total + after) * 0.5)
        grad_y = grads[2] + (after - before) * 0.5
        lit = lighting(grad_z, grad_x, grad_y)
        sums = [jnp.sum(weight * lit, axis=0, keepdims=True) for weight in weights]
        return [total + trade(total, lane[:1], width) for total in sums]

    def row_of(ref, row):
        return [ref[part, :, row, :] for part in range(3)]

    row = lax.broadcasted_iota(jnp.int32, (ROWS, width), 0)
    image = [image_ref[c][:, :width] for c in range(3)]
    if paired:
        first = lax.axis_index("gx") == 0
        pick = lambda ref: [
            jnp.where(first, high, low) for high, low in zip(row_of(ref, ROWS - 1), row_of(ref, 0))
        ]
        sign = jnp.where(first, 1.0, -1.0)
        done = outermost(edge_refs[0], pick(grad_ref), pick(weight_ref), sign)
        place = jnp.where(first, ROWS - 1, 0)
        for c in range(3):
            out_ref[c] = jnp.where(row == place, done[c][:, :width], image[c])
    else:
        low = outermost(edge_refs[0], row_of(grad_ref, 0), row_of(weight_ref, 0), -1.0)
        last = ROWS - 1
        high = outermost(edge_refs[1], row_of(grad_ref, last), row_of(weight_ref, last), 1.0)
        for c in range(3):
            value = jnp.where(row == 0, low[c][:, :width], image[c])
            out_ref[c] = jnp.where(row == last, high[c][:, :width], value)
    out_ref[3] = image_ref[3][:, :width]


def staged_body(density, tf_index, tf_table):
    bricks, groups = lax.axis_size("depth"), len(FAR)
    layers, rows, length = density.shape
    width = length // bricks
    step_len = 1.0 / (layers * bricks)
    half = bricks // 2

    def call(kernel, out_shape, operands, scratch=(), cost=None, spec=WHOLE):
        return pl.pallas_call(
            kernel,
            out_shape=out_shape,
            in_specs=[spec] * len(operands),
            out_specs=jax.tree.map(lambda _: WHOLE, out_shape),
            scratch_shapes=scratch,
            cost_estimate=cost,
            compiler_params=PARAMS,
        )(*operands)

    def block(*shape):
        return jax.ShapeDtypeStruct(shape + (ROWS, LANES), jnp.float32)

    def swap(value, mask):
        return lax.ppermute(value, "depth", [(i, i ^ mask) for i in range(bricks)])

    inputs = [pltpu.with_memory_space_constraint(a, pltpu.HBM) for a in (density, tf_index)]
    theirs = swap(density, 1)
    ours = call(
        load_kernel,
        block(groups, 7),
        inputs,
        [
            pltpu.VMEM(density.shape, density.dtype),
            pltpu.VMEM(tf_index.shape, tf_index.dtype),
            pltpu.SemaphoreType.DMA,
            pltpu.SemaphoreType.DMA,
        ],
        pl.CostEstimate(flops=1 << 20, bytes_accessed=1 << 21, transcendentals=0),
        pl.BlockSpec(memory_space=pltpu.HBM),
    )
    sent = call(
        first_kernel, [block(ROWS + 1)] * groups, [ours, theirs], [pltpu.VMEM((groups, 3, ROWS, LANES), jnp.float32)]
    )
    came = []
    for value, step in zip(sent, FAR):
        pairs = [(i, step[i % 2][i // 4] * 4 + i % 4) for i in range(bricks)]
        came.append(lax.ppermute(value, "depth", pairs) if step != FAR[-1] else value)
    edge = jax.ShapeDtypeStruct((2, half, LANES), jnp.float32)
    keep, index, send, near, across = call(
        second_kernel,
        [jax.ShapeDtypeStruct((half, BLOCK, LANES), jnp.float32), block(2, groups), block(2 * half + 1), edge, edge],
        came,
        [
            pltpu.VMEM((2, half, BLOCK, LANES), jnp.float32),
            pltpu.VMEM((2, 2, groups, ROWS, LANES), jnp.float32),
        ],
    )
    other = swap(send, 2)
    near = lax.ppermute(near, "gx", [(0, 1), (1, 0)])
    across = lax.ppermute(
        across, ("depth", "gx"), [(2 * i + g, 2 * (i ^ 2) + 1 - g) for i in range(bricks) for g in range(2)]
    )
    given = call(index_kernel, block(half), [index, other])
    given = swap(given, 1)
    voxels = block(3, bricks)
    parts = call(
        functools.partial(staged_render_kernel, width, step_len),
        [block(4), voxels, voxels],
        [keep, other, index, given, tf_table],
        [pltpu.VMEM((bricks, BLOCK, LANES), jnp.float32)],
        pl.CostEstimate(flops=1 << 24, bytes_accessed=1 << 23, transcendentals=0),
    )
    return call(
        functools.partial(staged_finish_kernel, width),
        jax.ShapeDtypeStruct((4, rows, width), jnp.float32),
        [*parts, across, near],
        [pltpu.VMEM((2, bricks, LANES), jnp.float32)],
    )


def body(density, tf_index, tf_table):
    bricks, ranks = lax.axis_size("depth"), lax.axis_size("gx")
    layers, rows, length = density.shape
    width = length // bricks
    if bricks == 16 and ranks == 2 and layers == 2 and rows == ROWS and 2 * width == LANES:
        return staged_body(density, tf_index, tf_table)
    assert layers == 2 and rows == ROWS and 2 * width <= LANES and LANES % width == 0
    step_len = 1.0 / (layers * bricks)
    edge = jax.ShapeDtypeStruct((2, bricks, LANES), jnp.float32)
    paired = ranks == 2
    inputs = [pltpu.with_memory_space_constraint(a, pltpu.HBM) for a in (density, tf_index)]
    landing = [
        pltpu.VMEM(density.shape, density.dtype),
        pltpu.VMEM(tf_index.shape, tf_index.dtype),
        pltpu.SemaphoreType.DMA,
        pltpu.SemaphoreType.DMA,
    ]
    packed = pl.pallas_call(
        functools.partial(pack_kernel, width),
        out_shape=jax.ShapeDtypeStruct((bricks, BLOCK, LANES), jnp.float32),
        in_specs=[pl.BlockSpec(memory_space=pltpu.HBM)] * 2,
        out_specs=WHOLE,
        scratch_shapes=landing,
        name="pack",
        compiler_params=PARAMS,
    )(*inputs)
    got = lax.all_to_all(packed, "depth", 0, 0, tiled=True)
    outer = pl.pallas_call(
        edge_pick_kernel if paired else edge_kernel,
        out_shape=[edge] * (1 if paired else 2),
        in_specs=[WHOLE],
        out_specs=[WHOLE] * (1 if paired else 2),
        name="edge",
        compiler_params=PARAMS,
    )(got)
    if paired:
        edges = [lax.ppermute(outer[0], "gx", [(0, 1), (1, 0)])]
    else:
        edges = [
            lax.ppermute(outer[1], "gx", [(i, i + 1) for i in range(ranks - 1)]),
            lax.ppermute(outer[0], "gx", [(i + 1, i) for i in range(ranks - 1)]),
        ]
    voxels = jax.ShapeDtypeStruct((3, bricks, ROWS, LANES), jnp.float32)
    parts = pl.pallas_call(
        functools.partial(render_kernel, width, step_len),
        out_shape=[jax.ShapeDtypeStruct((4, ROWS, LANES), jnp.float32), voxels, voxels],
        in_specs=[WHOLE] * 2,
        out_specs=[WHOLE] * 3,
        cost_estimate=pl.CostEstimate(flops=1 << 24, bytes_accessed=1 << 23, transcendentals=0),
        name="render",
        compiler_params=PARAMS,
    )(got, tf_table)
    return pl.pallas_call(
        functools.partial(finish_kernel, width, paired),
        out_shape=jax.ShapeDtypeStruct((4, rows, width), jnp.float32),
        in_specs=[WHOLE] * (3 + len(edges)),
        out_specs=WHOLE,
        name="finish",
        compiler_params=PARAMS,
    )(*parts, *edges)


def solution(mesh):
    in_specs = (P("depth", "gx", None), P("depth", "gx", None), P())
    out_specs = P(None, "gx", "depth")
    return jax.shard_map(body, mesh=mesh, in_specs=in_specs, out_specs=out_specs, check_vma=False)
```
